32 devices in a mesh: dp: 8 (over z, x), row: 2 (over y), col: 2 (over core).
Axes of the slice: x: 2, y: 2, z: 4, core: 2. Of those that a mesh axis runs over, the one named last changes fastest.
Arguments:
- block_input: bfloat16 [6272, 512], P('dp', 'row'), may hold values from -6 to 6
- out_grad: bfloat16 [6272, 512], P('dp', 'row'), may hold values from -6 to 6
- first_gain: float32 [512], P('row'), may hold values from 0.5 to 1.5
- first_shift: float32 [512], P('row'), may hold values from -3 to 3
- qkv_weight: bfloat16 [512, 3, 512], P('row', None, 'col'), may hold values from -0.25 to 0.25
- query_bias: float32 [512], P('col'), may hold values from -3 to 3
- value_bias: float32 [512], P('col'), may hold values from -0.6 to 0.6
- position_table: float32 [169, 16], P(None, 'col'), may hold values from -6 to 306
- position_index: int32 [49, 49], replicated, may hold values from 0 to 168
- proj_weight: bfloat16 [512, 512], P('col', 'row'), may hold values from -2 to 2
- proj_bias: float32 [512], P('row'), may hold values from -1.2 to 1.2
- second_gain: float32 [512], P('row'), may hold values from 0.5 to 1.5
- second_shift: float32 [512], P('row'), may hold values from -3 to 3
- expand_weight: bfloat16 [512, 2048], P('row', 'col'), may hold values from -0.5 to 0.5
- expand_bias: float32 [2048], P('col'), may hold values from -3 to 3
- reduce_weight: bfloat16 [2048, 512], P('col', 'row'), may hold values from -0.5 to 0.5
- reduce_bias: float32 [512], P('row'), may hold values from -3 to 3
Outputs:
- block_output: bfloat16 [6272, 512], P('dp', 'row')
- input_grad: float32 [6272, 512], P('dp', 'row')
- first_gain_grad: float32 [512], P('row')
- first_shift_grad: float32 [512], P('row')
- qkv_weight_grad: float32 [512, 3, 512], P('row', None, 'col')
- query_bias_grad: float32 [512], P('col')
- value_bias_grad: float32 [512], P('col')
- position_table_grad: float32 [169, 16], P(None, 'col')
- proj_weight_grad: float32 [512, 512], P('col', 'row')
- proj_bias_grad: float32 [512], P('row')
- second_gain_grad: float32 [512], P('row')
- second_shift_grad: float32 [512], P('row')
- expand_weight_grad: float32 [512, 2048], P('row', 'col')
- expand_bias_grad: float32 [2048], P('col')
- reduce_weight_grad: float32 [2048, 512], P('col', 'row')
- reduce_bias_grad: float32 [512], P('row')
The draws below stay inside these ranges and needn't reach their ends.
Inputs may be any that keep to these rules, and one draw needn't show every extreme that they name: `position_index`: entries name rows of position_table.
All inputs are finite; a program needn't handle non-finite values.
Results may differ from the reference program's by a relative error of at most 0.012.
The reference program's roundings to bfloat16 on the way count: a program that leaves them out, or rounds other values in their place, can miss the bound.
Values may be sent and summed in bfloat16 or wider, within the bound.
A program may use at most 64 MiB of HBM per device.

```python
import math
import jax
import jax.numpy as jnp
from jax import lax

WIDTH = 512
HEADS = 16
MLP_WIDTH = 2048
WINDOW = 49
TABLE = 169
TOKENS = 6272


def draw_position_table(key, part):
    base_key = jax.random.fold_in(key, 0)
    table = jnp.clip(jax.random.normal(base_key, (TABLE, HEADS), jnp.float32), -6.0, 6.0)
    return table


def set_ends(drawn, own_key, low, top_value):
    spot = [jax.random.randint(jax.random.fold_in(own_key, axis), (), 0, length) for axis, length in enumerate(drawn.shape)]
    longest = drawn.shape.index(max(drawn.shape))
    beside = spot[:longest] + [(spot[longest] + 1) % drawn.shape[longest]] + spot[longest + 1:]
    return drawn.at[tuple(spot)].set(low).at[tuple(beside)].set(top_value)


def shard_levels(own_key, extent, cuts, least, high):
    loudness, own = 1.0, jax.random.fold_in(own_key, 6)
    for position, shards_of in cuts:
        heights = jnp.exp(jax.random.uniform(jax.random.fold_in(own, position), (shards_of,), jnp.float32, least / len(cuts), high / len(cuts)))
        loudness = loudness * jnp.repeat(heights, extent[position] // shards_of).reshape([-1 if axis == position else 1 for axis in range(len(extent))])
    return loudness


def noise(rng, dims, scale, bound, cuts=(), dtype=jnp.bfloat16):
    factor_of = shard_levels(rng, dims, cuts, -0.22, 0.18) if cuts else 1.0
    values = jax.random.normal(rng, dims, jnp.float32) * scale * factor_of
    return jnp.minimum(jnp.maximum(values, -bound), bound).astype(dtype)


def setup_inputs(seed: int = 0) -> dict:
    key_of = jax.random.split(jax.random.key(seed), 18)
    block_input = noise(key_of[0], (TOKENS, WIDTH), 1.0, 6.0, ((0, 8), (1, 2)))
    out_grad = noise(key_of[1], (TOKENS, WIDTH), 1.0, 6.0, ((0, 8), (1, 2)))
    first_gain = jnp.clip(1.0 + 0.1 * jax.random.normal(key_of[2], (WIDTH,), jnp.float32), 0.5, 1.5)
    first_shift = noise(key_of[3], (WIDTH,), 0.5, 3.0, ((0, 2),), jnp.float32)
    qkv_weight = noise(key_of[4], (WIDTH, 3, WIDTH), WIDTH ** -0.5, 0.25, ((0, 2), (2, 2)))
    query_bias = noise(key_of[5], (WIDTH,), 0.5, 3.0, ((0, 2),), jnp.float32)
    value_bias = noise(key_of[6], (WIDTH,), 0.1, 0.6, ((0, 2),), jnp.float32)
    position_table = draw_position_table(jax.random.fold_in(key_of[17], 71), 0)
    position_index = set_ends(jax.random.randint(key_of[8], (WINDOW, WINDOW), 0, TABLE), jax.random.fold_in(key_of[8], 1), 0, TABLE - 1).astype(jnp.int32)
    proj_weight = noise(key_of[9], (WIDTH, WIDTH), (WIDTH // 49) ** -0.5, 2.0, ((0, 2), (1, 2)))
    proj_bias = noise(key_of[10], (WIDTH,), 0.2, 1.2, ((0, 2),), jnp.float32)
    second_gain = jnp.clip(1.0 + 0.1 * jax.random.normal(key_of[11], (WIDTH,), jnp.float32), 0.5, 1.5)
    second_shift = noise(key_of[12], (WIDTH,), 0.5, 3.0, ((0, 2),), jnp.float32)
    expand_weight = noise(key_of[13], (WIDTH, MLP_WIDTH), (WIDTH // 4) ** -0.5, 0.5, ((0, 2), (1, 2)))
    expand_bias = noise(key_of[14], (MLP_WIDTH,), 0.5, 3.0, ((0, 2),), jnp.float32)
    reduce_weight = noise(key_of[15], (MLP_WIDTH, WIDTH), (MLP_WIDTH // 16) ** -0.5, 0.5, ((0, 2), (1, 2)))
    reduce_bias = noise(key_of[16], (WIDTH,), 0.5, 3.0, ((0, 2),), jnp.float32)
    return dict(block_input=block_input, out_grad=out_grad, first_gain=first_gain, first_shift=first_shift, qkv_weight=qkv_weight, query_bias=query_bias, value_bias=value_bias, position_table=position_table, position_index=position_index, proj_weight=proj_weight, proj_bias=proj_bias, second_gain=second_gain, second_shift=second_shift, expand_weight=expand_weight, expand_bias=expand_bias, reduce_weight=reduce_weight, reduce_bias=reduce_bias)


EPSILON = 1e-05
ROOT_HALF = 0.7071067811865476
GAUSS_PEAK = 0.3989422804014327

def rounded(tensor):
    return lax.optimization_barrier(tensor.astype(jnp.bfloat16))

def to_windows(tokens):
    features = tokens.shape[-1]
    halves = tokens.shape[0] // 98
    shaped = tokens.reshape(halves, 7, 2, 7, features).transpose(0, 2, 1, 3, 4)
    return shaped.reshape(halves * 2, 49, features)

def from_windows(windows):
    features = windows.shape[-1]
    halves = windows.shape[0] // 2
    shaped = windows.reshape(halves, 2, 7, 7, features).transpose(0, 2, 1, 3, 4)
    return shaped.reshape(halves * 98, features)

def split_heads(tokens, head_count):
    windows = to_windows(tokens)
    return windows.reshape(windows.shape[0], 49, head_count, windows.shape[2] // head_count)

def merge_heads(windows):
    merged = windows.reshape(windows.shape[0], 49, windows.shape[2] * windows.shape[3])
    return from_windows(merged)

def gelu_value(pre_act):
    return 0.5 * pre_act * (1.0 + jax.scipy.special.erf(pre_act * ROOT_HALF))

def gelu_slope(pre_act):
    return 0.5 * (1.0 + jax.scipy.special.erf(pre_act * ROOT_HALF)) + pre_act * GAUSS_PEAK * jnp.exp(-0.5 * pre_act * pre_act)

def norm_forward(values):
    center = lax.optimization_barrier(jnp.mean(values, axis=-1, keepdims=True))
    shifted = values - center
    spread = lax.optimization_barrier(jnp.mean(shifted * shifted, axis=-1, keepdims=True))
    inverse = lax.rsqrt(spread + EPSILON)
    return (shifted * inverse, inverse)

def norm_backward(upstream, gain, normed, inverse):
    scaled = upstream * gain
    grad_mean = lax.optimization_barrier(jnp.mean(scaled, axis=-1, keepdims=True))
    grad_corr = lax.optimization_barrier(jnp.mean(scaled * normed, axis=-1, keepdims=True))
    return inverse * (scaled - grad_mean - normed * grad_corr)

def layer_block(block_rows, grad_rows, weights, pos_bias):
    first_gain, first_shift, qkv_weight, query_bias, value_bias, proj_weight, proj_bias, second_gain, second_shift, expand_weight, expand_bias, reduce_weight, reduce_bias = weights
    full_width = block_rows.shape[1]
    head_count = pos_bias.shape[0]
    score_scale = (full_width // head_count) ** (-0.5)
    inputs = block_rows.astype(jnp.float32)
    normed_one, inverse_one = norm_forward(inputs)
    ln_one = rounded(normed_one * first_gain + first_shift)
    flat_weight = qkv_weight.reshape(full_width, 3 * full_width)
    linear = jnp.dot(ln_one, flat_weight, preferred_element_type=jnp.float32).reshape(-1, 3, full_width)
    bias_rows = jnp.stack([query_bias, jnp.zeros_like(query_bias), value_bias])
    linear = linear + bias_rows[None]
    queries = rounded(linear[:, 0] * score_scale)
    key_rows = rounded(linear[:, 1])
    value_rows = rounded(linear[:, 2])
    query_heads = split_heads(queries, head_count).astype(jnp.float32)
    key_heads = split_heads(key_rows, head_count).astype(jnp.float32)
    value_heads = split_heads(value_rows, head_count).astype(jnp.float32)
    scores = jnp.einsum('wihd,wjhd->whij', query_heads, key_heads) + pos_bias[None]
    row_top = lax.optimization_barrier(jnp.max(scores, axis=-1, keepdims=True))
    log_total = row_top + jnp.log(lax.optimization_barrier(jnp.sum(jnp.exp(scores - row_top), axis=-1, keepdims=True)))
    probs = jnp.exp(scores - log_total)
    probs_b = rounded(probs).astype(jnp.float32)
    mixed = rounded(merge_heads(jnp.einsum('whij,wjhd->wihd', probs_b, value_heads)))
    middle = inputs + jnp.dot(mixed, proj_weight, preferred_element_type=jnp.float32) + proj_bias
    normed_two, inverse_two = norm_forward(middle)
    ln_two = rounded(normed_two * second_gain + second_shift)
    pre_act = jnp.dot(ln_two, expand_weight, preferred_element_type=jnp.float32) + expand_bias
    hidden = rounded(gelu_value(pre_act))
    block_out = (middle + jnp.dot(hidden, reduce_weight, preferred_element_type=jnp.float32) + reduce_bias).astype(jnp.bfloat16)
    upstream = grad_rows.astype(jnp.float32)
    reduce_w_grad = jnp.dot(hidden.T, grad_rows, preferred_element_type=jnp.float32)
    reduce_b_grad = lax.optimization_barrier(jnp.sum(upstream, axis=0))
    hidden_grad = jnp.dot(grad_rows, reduce_weight.T, preferred_element_type=jnp.float32)
    pre_grad = rounded(hidden_grad * gelu_slope(pre_act))
    expand_b_grad = lax.optimization_barrier(jnp.sum(pre_grad.astype(jnp.float32), axis=0))
    expand_w_grad = jnp.dot(ln_two.T, pre_grad, preferred_element_type=jnp.float32)
    second_grad = jnp.dot(pre_grad, expand_weight.T, preferred_element_type=jnp.float32)
    second_gain_grad = lax.optimization_barrier(jnp.sum(second_grad * normed_two, axis=0))
    second_shift_grad = lax.optimization_barrier(jnp.sum(second_grad, axis=0))
    middle_grad = upstream + norm_backward(second_grad, second_gain, normed_two, inverse_two)
    middle_b = rounded(middle_grad)
    proj_w_grad = jnp.dot(mixed.T, middle_b, preferred_element_type=jnp.float32)
    proj_b_grad = lax.optimization_barrier(jnp.sum(middle_grad, axis=0))
    mixed_grad = rounded(jnp.dot(middle_b, proj_weight.T, preferred_element_type=jnp.float32))
    grad_heads = split_heads(mixed_grad, head_count).astype(jnp.float32)
    prob_grad = jnp.einsum('wihd,wjhd->whij', grad_heads, value_heads)
    value_grad = jnp.einsum('whij,wihd->wjhd', probs_b, grad_heads)
    centre = lax.optimization_barrier(jnp.sum(probs * prob_grad, axis=-1, keepdims=True))
    score_grad = probs * (prob_grad - centre)
    bias_grad = lax.optimization_barrier(jnp.sum(score_grad, axis=0))
    score_b = rounded(score_grad).astype(jnp.float32)
    query_grad = jnp.einsum('whij,wjhd->wihd', score_b, key_heads) * score_scale
    key_grad = jnp.einsum('whij,wihd->wjhd', score_b, query_heads)
    linear_grad = jnp.stack([merge_heads(query_grad), merge_heads(key_grad), merge_heads(value_grad)], axis=1)
    query_b_grad = lax.optimization_barrier(jnp.sum(linear_grad[:, 0], axis=0))
    value_b_grad = lax.optimization_barrier(jnp.sum(linear_grad[:, 2], axis=0))
    linear_b = rounded(linear_grad).reshape(-1, 3 * full_width)
    qkv_grad = jnp.dot(ln_one.T, linear_b, preferred_element_type=jnp.float32).reshape(full_width, 3, full_width)
    first_grad = jnp.dot(linear_b, flat_weight.T, preferred_element_type=jnp.float32)
    first_gain_grad = lax.optimization_barrier(jnp.sum(first_grad * normed_one, axis=0))
    first_shift_grad = lax.optimization_barrier(jnp.sum(first_grad, axis=0))
    input_grad = middle_grad + norm_backward(first_grad, first_gain, normed_one, inverse_one)
    grads = (first_gain_grad, first_shift_grad, qkv_grad, query_b_grad, value_b_grad, bias_grad, proj_w_grad, proj_b_grad, second_gain_grad, second_shift_grad, expand_w_grad, expand_b_grad, reduce_w_grad, reduce_b_grad)
    return (block_out, input_grad, grads)

def reference(block_input, out_grad, first_gain, first_shift, qkv_weight, query_bias, value_bias, position_table, position_index, proj_weight, proj_bias, second_gain, second_shift, expand_weight, expand_bias, reduce_weight, reduce_bias):
    weights = (first_gain, first_shift, qkv_weight, query_bias, value_bias, proj_weight, proj_bias, second_gain, second_shift, expand_weight, expand_bias, reduce_weight, reduce_bias)
    pos_bias = position_table[position_index].transpose(2, 0, 1)
    images = block_input.shape[0] // 196
    group_size = math.gcd(images, 16)
    block_rows = group_size * 196
    block_count = images // group_size
    inputs = block_input.reshape(block_count, block_rows, block_input.shape[1])
    grads_in = out_grad.reshape(block_count, block_rows, out_grad.shape[1])
    zero_grads = tuple((jnp.zeros(tensor.shape, jnp.float32) for tensor in weights[:5])) + (jnp.zeros(pos_bias.shape, jnp.float32),) + tuple((jnp.zeros(tensor.shape, jnp.float32) for tensor in weights[5:]))

    def one_block(totals, sample):
        block_out, input_grad, grads = layer_block(sample[0], sample[1], weights, pos_bias)
        return (jax.tree.map(jnp.add, totals, grads), (block_out, input_grad))
    total_grads, (outputs, input_grads) = lax.scan(one_block, zero_grads, (inputs, grads_in))
    head_count = position_table.shape[1]
    table_grad = jnp.zeros(position_table.shape, jnp.float32).at[position_index.reshape(-1)].add(total_grads[5].transpose(1, 2, 0).reshape(-1, head_count))
    return (outputs.reshape(block_input.shape), input_grads.reshape(block_input.shape), total_grads[0], total_grads[1], total_grads[2], total_grads[3], total_grads[4], table_grad, total_grads[6], total_grads[7], total_grads[8], total_grads[9], total_grads[10], total_grads[11], total_grads[12], total_grads[13])
```

```python
import functools
from types import SimpleNamespace

import jax
import jax.numpy as jnp
from jax import lax
from jax.experimental import pallas as pl
from jax.experimental.pallas import tpu as pltpu
from jax.sharding import PartitionSpec as P

EPSILON = 1e-05
ROOT_HALF = 0.7071067811865476
GAUSS_PEAK = 0.3989422804014327
SIDE = 7
WINDOW = SIDE * SIDE
IMAGE = 4 * WINDOW
TOK = 208
PAD = 64
ROWS = 4 * PAD
F32 = jnp.float32
BF16 = jnp.bfloat16
VMEM = pl.BlockSpec(memory_space=pltpu.VMEM)
MESH = pl.DeviceIdType.MESH
LIMIT = 60 * 1024 * 1024


def dot(left, right):
    return jnp.dot(left, right, preferred_element_type=F32)


def dot_t(left, right):
    return lax.dot_general(left, right, (((1,), (1,)), ((), ())), preferred_element_type=F32)


def t_dot(left, right):
    return lax.dot_general(left, right, (((0,), (0,)), ((), ())), preferred_element_type=F32)


def thirds(values):
    high = values.astype(BF16)
    rest = values - high.astype(F32)
    middle = rest.astype(BF16)
    return high, middle, (rest - middle.astype(F32)).astype(BF16)


def norm(values):
    center = jnp.mean(values, axis=-1, keepdims=True)
    shifted = values - center
    spread = jnp.mean(shifted * shifted, axis=-1, keepdims=True)
    inverse = lax.rsqrt(spread + EPSILON)
    return shifted * inverse, inverse


def norm_backward(upstream, gain, normed, inverse):
    scaled = upstream * gain
    return inverse * (
        scaled
        - jnp.mean(scaled, axis=-1, keepdims=True)
        - normed * jnp.mean(scaled * normed, axis=-1, keepdims=True)
    )


def head_mask(heads, width):
    size = width // heads
    head = lax.broadcasted_iota(jnp.int32, (heads, 1, width), 0)
    lane = lax.broadcasted_iota(jnp.int32, (heads, 1, width), 2)
    return (lane >= head * size) & (lane < (head + 1) * size)


def stack_heads(rows, mask):
    heads = mask.shape[0]
    wide = jnp.where(mask, rows.astype(F32)[None], 0.0)
    return wide.reshape(heads * rows.shape[0], rows.shape[1]).astype(BF16)


def fold_heads(stacked, mask):
    heads = mask.shape[0]
    split = stacked.reshape(heads, stacked.shape[0] // heads, stacked.shape[1])
    return jnp.sum(jnp.where(mask, split, 0.0), axis=0)


def softmax(scores):
    top = jnp.max(scores, axis=-1, keepdims=True)
    powers = jnp.exp(scores - top)
    return powers / jnp.sum(powers, axis=-1, keepdims=True)


def block_kernel(n, size, names, *refs):
    r = SimpleNamespace(**dict(zip(names, refs)))
    me = lax.axis_index("dp")
    row, col = lax.axis_index("row"), lax.axis_index("col")
    cores = lax.axis_size("col")
    parity, place = lax.rem(me, 2), me // 2
    peers = n // 2
    over_col, over_row = {"col": 1 - col}, {"row": 1 - row}
    pair = {"dp": me + 1 - 2 * parity}
    half, width, hid = r.x_in.shape[1], r.wp.shape[0], r.we.shape[1]
    heads = r.table.shape[1]
    scale = (width // heads) ** (-0.5)
    images = r.x_in.shape[0] // IMAGE
    slices = hid // half
    full = 2 * half
    mine = row * cores + col
    theirs = (1 - row) * cores + col
    wide, block = size // 2, size // n
    chunks = r.o_f.shape[0] // size
    live = {}

    def peer_of(k):
        there = lax.rem(place + k, peers)
        return there, {"dp": 2 * there + parity}

    barrier = pltpu.get_barrier_semaphore()
    for device in [over_col, over_row, pair] + [peer_of(k)[1] for k in range(1, peers)]:
        pl.semaphore_signal(barrier, inc=1, device_id=device, device_id_type=MESH)

    def start(key, src, dst, device):
        index = len(live)
        live[key] = pltpu.make_async_remote_copy(
            src, dst, r.sems.at[0, index], r.sems.at[1, index], device, MESH
        )
        live[key].start()

    def arrived(*key):
        live[key].wait_recv()

    def tokens_of(image):
        return pl.ds(pl.multiple_of(image * TOK, 16), TOK)

    spot = lax.broadcasted_iota(jnp.int32, (TOK, images * IMAGE), 1)
    line = lax.broadcasted_iota(jnp.int32, (TOK, images * IMAGE), 0)
    line = jnp.where(line < IMAGE, line, -IMAGE * images)
    for k in range(images):
        r.sel[k * TOK:(k + 1) * TOK] = jnp.where(spot == line + k * IMAGE, 1.0, 0.0).astype(BF16)
    place_in = lax.broadcasted_iota(jnp.int32, (ROWS, TOK), 0)
    spot = lax.broadcasted_iota(jnp.int32, (ROWS, TOK), 1)
    window, i = place_in >> 6, place_in & (PAD - 1)
    i_row = (i * 37) >> 8
    target = ((window >> 1) * SIDE + i_row) * (2 * SIDE) + (window & 1) * SIDE + i - SIDE * i_row
    target = jnp.where(i < WINDOW, target, -1)
    r.perm[...] = jnp.where(spot == target, 1.0, 0.0).astype(BF16)
    sel_mine, sel_theirs = r.sel[tokens_of(mine)], r.sel[tokens_of(theirs)]
    r.x_away[...] = dot(sel_theirs, r.x_in[...]).astype(BF16)
    r.g_away[...] = dot(sel_theirs, r.g_in[...]).astype(BF16)
    r.vec_own[...] = jnp.zeros_like(r.vec_own)
    r.cvec_own[...] = jnp.zeros_like(r.cvec_own)
    for k, ref in enumerate((r.gain1, r.shift1, r.bias_p, r.gain2, r.shift2, r.bias_r)):
        r.vec_own[k:k + 1] = ref[...]
    r.cvec_own[0:1] = r.bias_q[...]
    r.cvec_own[1:2] = r.bias_v[...]
    for k in range(slices):
        r.cvec_own[2 + k:3 + k] = r.bias_e[:, k * half:(k + 1) * half]
    pl.semaphore_wait(barrier, peers + 2)

    weights = {
        "q": (r.wq, r.q_xo, r.q_ox, r.q_xx, 2),
        "p": (r.wp, r.p_xo, r.p_ox, r.p_xx, 1),
        "e": (r.we, r.e_xo, r.e_ox, r.e_xx, 2),
        "r": (r.wr, r.r_xo, r.r_ox, r.r_xx, 2),
    }

    def pieces(name, side):
        rows, count = weights[name][0].shape[0], weights[name][4]
        step = rows // (2 * count)
        for p in range(count):
            yield p, pl.ds(pl.multiple_of(side * (rows // 2) + p * step, step), step)

    def fetch(name):
        oo, xo, ox, _, _ = weights[name]
        for p, rows in pieces(name, parity):
            start((name, "y", p), oo.at[rows], xo.at[rows], over_row)
        start((name, "c"), oo, ox, over_col)

    def relay(name):
        _, xo, _, xx, _ = weights[name]
        for p, rows in pieces(name, parity):
            arrived(name, "y", p)
            start((name, "x", p), xo.at[rows], xo.at[rows], pair)
            start((name, "cy", p), xo.at[rows], xx.at[rows], over_col)

    def relay_back(name):
        _, xo, _, xx, _ = weights[name]
        for p, rows in pieces(name, 1 - parity):
            arrived(name, "x", p)
            start((name, "cx", p), xo.at[rows], xx.at[rows], over_col)

    def ready(name):
        arrived(name, "c")
        for p in range(weights[name][4]):
            arrived(name, "cy", p)
            arrived(name, "cx", p)

    start(("x",), r.x_away, r.x_oth, over_row)
    start(("vec",), r.vec_own, r.vec_oth, over_row)
    start(("cvec",), r.cvec_own, r.cvec_oth, over_col)
    fetch("q")
    fetch("p")
    fetch("e")
    start(("g",), r.g_away, r.g_oth, over_row)
    fetch("r")

    entries = r.table.shape[0]
    which = lax.broadcasted_iota(jnp.int32, (entries, WINDOW * PAD), 0)
    r.hot[...] = jnp.where(which == r.index[...], 1.0, 0.0).astype(BF16)
    spread = sum(t_dot(part, r.hot[...]) for part in thirds(r.table[...]))
    lane = lax.broadcasted_iota(jnp.int32, (heads, PAD), 1)
    r.b_own[...] = jnp.zeros_like(r.b_own)
    for k in range(WINDOW):
        r.b_own[pl.ds(k, heads, stride=PAD), :] = jnp.where(
            lane < WINDOW, spread[:, k * PAD:(k + 1) * PAD], -1e30
        )
    start(("bias",), r.b_own, r.b_oth, over_col)
    x_own = dot(sel_mine, r.x_in[...]).astype(BF16)
    grad_own = dot(sel_mine, r.g_in[...]).astype(BF16)
    mask = head_mask(heads, width)

    arrived("x")
    arrived("vec")
    rvec = jnp.concatenate([r.vec_own[...], r.vec_oth[...]], axis=1)
    x = dot(r.perm[...], jnp.concatenate([x_own, r.x_oth[...]], axis=1))
    normed, inverse_one = norm(x)
    r.n_one[...] = normed
    r.ln_one[...] = (normed * rvec[0:1] + rvec[1:2]).astype(BF16)
    relay("q")
    relay_back("q")
    relay("p")
    arrived("cvec")
    q_side = (r.wq, r.q_ox), (r.q_xo, r.q_xx)
    p_side = (r.wp, r.p_ox), (r.p_xo, r.p_xx)
    e_side = (r.we, r.e_ox), (r.e_xo, r.e_xx)
    r_side = (r.wr, r.r_ox), (r.r_xo, r.r_xx)
    bias_refs = (r.b_own, r.b_oth)
    cvecs = (r.cvec_own, r.cvec_oth)
    step_of = {(0, 1): ("relay_back", "p"), (0, 3): ("relay", "e"), (1, 1): ("relay_back", "e"), (1, 2): ("relay", "r")}
    for b in range(2):
        cols = slice(b * width, (b + 1) * width)
        if b == 1:
            ready("q")
            arrived("bias")
        for s, out in enumerate((r.q, r.k, r.v)):
            part = slice(s * width, (s + 1) * width)
            linear = dot(r.ln_one[:, :half], q_side[0][b][:, part]) + dot(
                r.ln_one[:, half:], q_side[1][b][:, part]
            )
            if s == 0:
                linear = (linear + cvecs[b][0:1]) * scale
            if s == 2:
                linear = linear + cvecs[b][1:2]
            out[:, cols] = linear.astype(BF16)
        for w in range(4):
            rows = slice(w * PAD, (w + 1) * PAD)
            scores = dot_t(stack_heads(r.q[rows, cols], mask), r.k[rows, cols]) + bias_refs[b][...]
            probs = softmax(scores)
            r.probs[b * 4 + w] = probs
            r.mixed[rows, cols] = fold_heads(dot(probs.astype(BF16), r.v[rows, cols]), mask).astype(BF16)
            if (b, w) in step_of:
                what, name = step_of[b, w]
                (relay if what == "relay" else relay_back)(name)
    ready("p")
    parts = [
        dot(r.mixed[:, :width], p_side[a][0][...]) + dot(r.mixed[:, width:], p_side[a][1][...])
        for a in range(2)
    ]
    middle = x + jnp.concatenate(parts, axis=1) + rvec[2:3]
    r.middle[...] = middle
    normed_two, inverse_two = norm(middle)
    r.ln_two[...] = (normed_two * rvec[3:4] + rvec[4:5]).astype(BF16)
    relay_back("r")
    arrived("g")
    grad = dot(r.perm[...], jnp.concatenate([grad_own, r.g_oth[...]], axis=1))
    r.grad[...] = grad.astype(BF16)
    ready("e")
    ready("r")

    def rows_of(c):
        return slice(c * size, (c + 1) * size)

    begun, rowed = [0], [0]

    def away_done(blocks):
        while (begun[0] + 1) * size <= blocks * half:
            c = begun[0]
            start(("y", c), r.y_b.at[rows_of(c)], r.yr.at[rows_of(c)], over_col)
            start(("z", c), r.z_b.at[rows_of(c)], r.zr.at[rows_of(c)], over_col)
            begun[0] += 1

    def home_done(blocks):
        while (rowed[0] + 1) * size <= blocks * half:
            c = rowed[0]
            rows = rows_of(c)
            arrived("z", c)
            r.xb[rows] = (r.x_f[rows] + r.zr[rows].astype(F32)).astype(BF16)
            start(("r", c), r.xb.at[rows], r.xr.at[rows], over_row)
            rowed[0] += 1

    def stage_pair(c):
        arrived("y", c)
        arrived("r", c)
        rows = rows_of(c)
        r.sf[...] = r.o_f[rows] + r.yr[rows].astype(F32) + r.xr[rows].astype(F32)
        r.sb[rows] = r.sf[...].astype(BF16)
        r.tf[c] = r.sf[pl.ds(pl.multiple_of(parity * wide, wide), wide)]
        away = pl.ds(pl.multiple_of(c * size + (1 - parity) * wide, wide), wide)
        start(("p", c), r.sb.at[away], r.pr.at[c], pair)

    def stage_rest(c):
        arrived("p", c)
        r.tf[c] = r.tf[c] + r.pr[c].astype(F32)
        r.tb[c] = r.tf[c].astype(BF16)
        for k in range(1, peers):
            there, device = peer_of(k)
            piece = pl.ds(pl.multiple_of(there * block, block), block)
            start(("q", c, k), r.tb.at[c, piece], r.qr.at[c, k], device)

    def stage_sum(c):
        total = r.tf[c, pl.ds(pl.multiple_of(place * block, block), block)]
        for k in range(1, peers):
            arrived("q", c, k)
            total = total + r.qr[c, k].astype(F32)
        own = pl.ds(pl.multiple_of(c * size + parity * wide + place * block, block), block)
        r.gb[own] = total.astype(BF16)
        for k in range(1, peers):
            start(("g", c, k), r.gb.at[own], r.gb.at[own], peer_of(k)[1])

    def stage_back(c):
        for k in range(1, peers):
            arrived("g", c, k)
        part = pl.ds(pl.multiple_of(c * size + parity * wide, wide), wide)
        start(("b", c), r.gb.at[part], r.gb.at[part], pair)

    def stage_out(c):
        arrived("b", c)
        for at in range(c * size // half, (c + 1) * size // half):
            rows = slice(at * half, (at + 1) * half)
            values = r.gb[rows].astype(F32)
            if at < 2 * slices:
                here = slice(at // 2 * half, (at // 2 + 1) * half)
                if at % 2 == 0:
                    r.out_e[:, here] = values
                else:
                    r.out_r[here] = values
            elif at == 2 * slices:
                r.out_p[...] = values
            else:
                s = at - 2 * slices - 1
                r.out_q[:, s * half:(s + 1) * half] = values

    stages = (stage_pair, stage_rest, stage_sum, stage_back, stage_out)
    stepped = [0]

    def tick():
        step = stepped[0]
        if step >= chunks + len(stages) - 1 or (step < chunks and step >= rowed[0]):
            return
        for k in reversed(range(len(stages))):
            if 0 <= step - k < chunks:
                stages[k](step - k)
        stepped[0] += 1

    homes, aways = (r.o_f, r.x_f), (r.y_b, r.z_b)
    r.small[...] = jnp.zeros_like(r.small)
    for q in range(slices):
        here = slice(q * half, (q + 1) * half)
        for b in (1, 0):
            cols = slice(b * hid + q * half, b * hid + (q + 1) * half)
            pre = dot(r.ln_two[:, :half], e_side[0][b][:, here]) + dot(
                r.ln_two[:, half:], e_side[1][b][:, here]
            )
            pre = pre + cvecs[b][2 + q:3 + q]
            erf_half = 0.5 * (1.0 + lax.erf(pre * ROOT_HALF))
            hidden = (pre * erf_half).astype(BF16)
            r.hidden[:, cols] = hidden
            slope = erf_half + pre * GAUSS_PEAK * jnp.exp(-0.5 * pre * pre)
            hgrad = dot_t(r.grad[:, :half], r_side[0][b][here]) + dot_t(
                r.grad[:, half:], r_side[1][b][here]
            )
            pgrad = (hgrad * slope).astype(BF16)
            r.pg[:, cols] = pgrad
            at = (32 if b == 0 else 16) + 2 + q
            r.small[at:at + 1] = jnp.sum(pgrad.astype(F32), axis=0, keepdims=True)
            up = slice(2 * q * half, (2 * q + 1) * half)
            down = slice((2 * q + 1) * half, (2 * q + 2) * half)
            for a, out in enumerate(homes if b == 0 else aways):
                side = slice(a * half, (a + 1) * half)
                out[up] = t_dot(r.ln_two[:, side], pgrad).astype(out.dtype)
                out[down] = t_dot(hidden, r.grad[:, side]).astype(out.dtype)
            if b == 1:
                away_done(2 * q + 2)
        home_done(2 * q + 2)
    second = jnp.concatenate(
        [
            dot_t(r.pg[:, :hid], e_side[a][0][...]) + dot_t(r.pg[:, hid:], e_side[a][1][...])
            for a in range(2)
        ],
        axis=1,
    )
    tick()
    mgrad = r.grad[...].astype(F32) + norm_backward(second, rvec[3:4], normed_two, inverse_two)
    r.mgrad[...] = mgrad
    r.mid_b[...] = mgrad.astype(BF16)
    for k, values in ((2, mgrad), (3, second * normed_two), (4, second), (5, r.grad[...].astype(F32))):
        total = jnp.sum(values, axis=0, keepdims=True)
        r.small[k:k + 1] = total[:, :half]
        r.small[8 + k:9 + k] = total[:, half:]
    base = 2 * slices * half
    for b in (1, 0):
        cols = slice(b * width, (b + 1) * width)
        r.mg[:, cols] = (
            dot_t(r.mid_b[:, :half], p_side[0][b][...]) + dot_t(r.mid_b[:, half:], p_side[1][b][...])
        ).astype(BF16)
        for a, out in enumerate(homes if b == 0 else aways):
            out[base:base + half] = t_dot(
                r.mixed[:, cols], r.mid_b[:, a * half:(a + 1) * half]
            ).astype(out.dtype)
    away_done(2 * slices + 1)

    def spread_out(key, values, out):
        tokens = t_dot(r.perm[...], values.astype(BF16)).astype(BF16)
        r.t_own[key] = tokens[:, :half]
        r.t_away[key] = tokens[:, half:]
        start(("o0", key), r.t_own.at[key], out.at[tokens_of(mine)], over_col)
        start(("o1", key), r.t_away.at[key], out.at[tokens_of(mine)], over_row)
        out[tokens_of(mine)] = tokens[:, :half]

    def pass_on(key, out):
        arrived("o1", key)
        start(("o2", key), out.at[tokens_of(theirs)], out.at[tokens_of(theirs)], over_col)

    def collect(key, out, result):
        arrived("o0", key)
        arrived("o2", key)
        result[...] = t_dot(r.sel[...], out[...]).astype(result.dtype)

    parts = [
        dot(r.hidden[:, :hid], r_side[a][0][...]) + dot(r.hidden[:, hid:], r_side[a][1][...])
        for a in range(2)
    ]
    home_done(2 * slices + 1)
    spread_out(0, r.middle[...] + jnp.concatenate(parts, axis=1) + rvec[5:6], r.t_blk)
    tick()

    for b in (1, 0):
        cols = slice(b * width, (b + 1) * width)
        small = 32 if b == 0 else 16
        q_sum = jnp.zeros((1, width), F32)
        v_sum = jnp.zeros((1, width), F32)
        for w in range(4):
            rows = slice(w * PAD, (w + 1) * PAD)
            keys, values = r.k[rows, cols], r.v[rows, cols]
            q_stack = stack_heads(r.q[rows, cols], mask)
            g_stack = stack_heads(r.mg[rows, cols], mask)
            probs = r.probs[b * 4 + w]
            pgrad = dot_t(g_stack, values)
            sgrad = probs * (pgrad - jnp.sum(probs * pgrad, axis=-1, keepdims=True))
            r.bg[b] = sgrad if w == 0 else r.bg[b] + sgrad
            score_b = sgrad.astype(BF16)
            q_grad = fold_heads(dot(score_b, keys), mask) * scale
            k_grad = t_dot(score_b, q_stack)
            v_grad = t_dot(probs.astype(BF16), g_stack)
            q_sum = q_sum + jnp.sum(q_grad, axis=0, keepdims=True)
            v_sum = v_sum + jnp.sum(v_grad, axis=0, keepdims=True)
            r.lin[b, rows, 0:width] = q_grad.astype(BF16)
            r.lin[b, rows, width:2 * width] = k_grad.astype(BF16)
            r.lin[b, rows, 2 * width:3 * width] = v_grad.astype(BF16)
            if w % 2 == 1:
                tick()
            if (b, w) == (1, 2):
                pass_on(0, r.t_blk)
        r.small[small:small + 1] = q_sum
        r.small[small + 1:small + 2] = v_sum
        for s in range(3):
            part = r.lin[b, :, s * width:(s + 1) * width]
            at = base + (s + 1) * half
            for a, out in enumerate(homes if b == 0 else aways):
                out[at:at + half] = t_dot(r.ln_one[:, a * half:(a + 1) * half], part).astype(out.dtype)
            if b == 1:
                away_done(2 * slices + 2 + s)
            else:
                home_done(2 * slices + 2 + s)
    tick()
    first = jnp.concatenate(
        [dot_t(r.lin[0], q_side[a][0][...]) + dot_t(r.lin[1], q_side[a][1][...]) for a in range(2)],
        axis=1,
    )
    for k, values in ((0, first * r.n_one[...]), (1, first)):
        total = jnp.sum(values, axis=0, keepdims=True)
        r.small[k:k + 1] = total[:, :half]
        r.small[8 + k:9 + k] = total[:, half:]
    for b in range(2):
        for k in range(0, WINDOW, 2):
            lines = [r.bg[b, pl.ds(k + i, heads, stride=PAD), :] for i in range(min(2, WINDOW - k))]
            r.flat[b * heads:(b + 1) * heads, k * PAD:(k + len(lines)) * PAD] = jnp.concatenate(lines, axis=1)
    table_grad = sum(dot_t(part, r.hot[...]) for part in thirds(r.flat[...]))
    r.small[40:48, 0:entries] = table_grad[:heads]
    r.small[24:32, 0:entries] = table_grad[heads:]
    start(("s0",), r.small.at[0:32], r.s_col, over_col)
    in_grad = r.mgrad[...] + norm_backward(first, rvec[0:1], r.n_one[...], inverse_one)
    spread_out(1, in_grad, r.t_in)
    tick()
    arrived("s0")
    r.s_mid[0:8] = r.small[8:16] + r.s_col[8:16]
    r.s_mid[8:24] = r.small[32:48] + r.s_col[16:32]
    start(("s1",), r.s_mid, r.s_row, over_row)
    collect(0, r.t_blk, r.out_b)
    tick()
    arrived("s1")
    r.s_pair[0:8] = r.small[0:8] + r.s_col[0:8] + r.s_row[0:8]
    r.s_pair[8:24] = r.s_mid[8:24] + r.s_row[8:24]
    start(("s2",), r.s_pair, r.s_other, pair)
    pass_on(1, r.t_in)
    tick()
    arrived("s2")
    r.s_dp[place] = r.s_pair[...] + r.s_other[...]
    for k in range(1, peers):
        start(("s3", k), r.s_dp.at[place], r.s_dp.at[place], peer_of(k)[1])
    tick()
    collect(1, r.t_in, r.out_x)
    tick()
    for k in range(1, peers):
        arrived("s3", k)
    acc = r.s_dp[0]
    for k in range(1, peers):
        acc = acc + r.s_dp[k]
    for k, ref in enumerate((r.o_gain1, r.o_shift1, r.o_bias_p, r.o_gain2, r.o_shift2, r.o_bias_r)):
        ref[...] = acc[k:k + 1]
    r.o_bias_q[...] = acc[8:9]
    r.o_bias_v[...] = acc[9:10]
    for k in range(slices):
        r.o_bias_e[:, k * half:(k + 1) * half] = acc[10 + k:11 + k]
    unit = jnp.where(
        lax.broadcasted_iota(jnp.int32, (heads, heads), 0)
        == lax.broadcasted_iota(jnp.int32, (heads, heads), 1),
        1.0,
        0.0,
    ).astype(BF16)
    turned = sum(t_dot(part, unit) for part in thirds(acc[16:16 + heads]))
    r.o_table[...] = turned[:entries]
    while stepped[0] < chunks + len(stages) - 1:
        tick()
    for key, copy in live.items():
        copy.wait_send()


def per_device(
    block_input, out_grad, first_gain, first_shift, qkv_weight, query_bias, value_bias,
    position_table, position_index, proj_weight, proj_bias, second_gain, second_shift,
    expand_weight, expand_bias, reduce_weight, reduce_bias,
):
    n = lax.axis_size("dp")
    half = block_input.shape[1]
    width = qkv_weight.shape[2]
    hid = expand_weight.shape[1]
    entries, heads = position_table.shape
    images = block_input.shape[0] // IMAGE
    full = 2 * half
    rows = 2 * hid + 4 * half
    size = max(n * 16, half)
    chunks, peers, wide = rows // size, n // 2, size // 2
    index = jnp.pad(position_index, ((0, 0), (0, PAD - WINDOW)), constant_values=-1).reshape(1, -1)
    inputs = dict(
        x_in=block_input, g_in=out_grad,
        gain1=first_gain[None], shift1=first_shift[None], bias_p=proj_bias[None],
        gain2=second_gain[None], shift2=second_shift[None], bias_r=reduce_bias[None],
        bias_q=query_bias[None], bias_v=value_bias[None], bias_e=expand_bias[None],
        table=position_table, index=index,
        wq=qkv_weight.reshape(half, 3 * width), wp=proj_weight, we=expand_weight, wr=reduce_weight,
    )
    outputs = dict(
        out_b=(block_input.shape, BF16), out_x=(block_input.shape, F32),
        out_q=((half, 3 * width), F32), out_p=((width, half), F32),
        out_e=((half, hid), F32), out_r=((hid, half), F32),
        o_gain1=((1, half), F32), o_shift1=((1, half), F32), o_bias_p=((1, half), F32),
        o_gain2=((1, half), F32), o_shift2=((1, half), F32), o_bias_r=((1, half), F32),
        o_bias_q=((1, width), F32), o_bias_v=((1, width), F32), o_bias_e=((1, hid), F32),
        o_table=((entries, heads), F32),
    )
    scratch = dict(
        sel=((images * TOK, images * IMAGE), BF16), perm=((ROWS, TOK), BF16),
        x_away=((TOK, half), BF16), x_oth=((TOK, half), BF16),
        g_away=((TOK, half), BF16), g_oth=((TOK, half), BF16),
        vec_own=((8, half), F32), vec_oth=((8, half), F32),
        cvec_own=((8, half), F32), cvec_oth=((8, half), F32),
        hot=((entries, WINDOW * PAD), BF16),
        b_own=((heads * PAD, PAD), F32), b_oth=((heads * PAD, PAD), F32),
        n_one=((ROWS, full), F32), ln_one=((ROWS, full), BF16),
        q=((ROWS, full), BF16), k=((ROWS, full), BF16), v=((ROWS, full), BF16),
        mixed=((ROWS, full), BF16), probs=((8, heads * PAD, PAD), F32),
        middle=((ROWS, full), F32), ln_two=((ROWS, full), BF16), grad=((ROWS, full), BF16),
        hidden=((ROWS, 2 * hid), BF16), pg=((ROWS, 2 * hid), BF16),
        mgrad=((ROWS, full), F32), mid_b=((ROWS, full), BF16), mg=((ROWS, full), BF16),
        lin=((2, ROWS, 3 * width), BF16), bg=((2, heads * PAD, PAD), F32),
        flat=((2 * heads, WINDOW * PAD), F32),
        t_own=((2, TOK, half), BF16), t_away=((2, TOK, half), BF16),
        t_blk=((images * TOK, half), BF16), t_in=((images * TOK, half), BF16),
        o_f=((rows, half), F32), x_f=((rows, half), F32),
        y_b=((rows, half), BF16), z_b=((rows, half), BF16),
        yr=((rows, half), BF16), zr=((rows, half), BF16),
        xb=((rows, half), BF16), xr=((rows, half), BF16), sb=((rows, half), BF16),
        gb=((rows, half), BF16), sf=((size, half), F32),
        pr=((chunks, wide, half), BF16), tb=((chunks, wide, half), BF16),
        tf=((chunks, wide, half), F32), qr=((chunks, peers, size // n, half), BF16),
        small=((48, half), F32), s_col=((32, half), F32), s_mid=((24, half), F32),
        s_row=((24, half), F32), s_pair=((24, half), F32), s_other=((24, half), F32),
        s_dp=((peers, 24, half), F32),
    )
    for name, weight in (("q", "wq"), ("p", "wp"), ("e", "we"), ("r", "wr")):
        for side in ("xo", "ox", "xx"):
            scratch[name + "_" + side] = (inputs[weight].shape, BF16)
    copies = 64 + chunks * (5 + 2 * (peers - 1)) + peers
    names = list(inputs) + list(outputs) + list(scratch) + ["sems"]
    results = pl.pallas_call(
        functools.partial(block_kernel, n, size, names),
        name="block",
        out_shape=tuple(jax.ShapeDtypeStruct(*out) for out in outputs.values()),
        in_specs=[VMEM] * len(inputs),
        out_specs=tuple([VMEM] * len(outputs)),
        scratch_shapes=[pltpu.VMEM(*shape) for shape in scratch.values()]
        + [pltpu.SemaphoreType.DMA((2, copies))],
        compiler_params=pltpu.CompilerParams(
            collective_id=0, has_side_effects=True, vmem_limit_bytes=LIMIT
        ),
    )(*inputs.values())
    got = dict(zip(outputs, results))
    return (
        got["out_b"], got["out_x"], got["o_gain1"][0], got["o_shift1"][0],
        got["out_q"].reshape(half, 3, width), got["o_bias_q"][0], got["o_bias_v"][0],
        got["o_table"], got["out_p"], got["o_bias_p"][0], got["o_gain2"][0], got["o_shift2"][0],
        got["out_e"], got["o_bias_e"][0], got["out_r"], got["o_bias_r"][0],
    )


def solution(mesh):
    in_specs = (
        P("dp", "row"), P("dp", "row"), P("row"), P("row"), P("row", None, "col"), P("col"),
        P("col"), P(None, "col"), P(), P("col", "row"), P("row"), P("row"), P("row"),
        P("row", "col"), P("col"), P("col", "row"), P("row"),
    )
    out_specs = (
        P("dp", "row"), P("dp", "row"), P("row"), P("row"), P("row", None, "col"), P("col"),
        P("col"), P(None, "col"), P("col", "row"), P("row"), P("row"), P("row"),
        P("row", "col"), P("col"), P("col", "row"), P("row"),
    )
    return jax.shard_map(
        per_device, mesh=mesh, in_specs=in_specs, out_specs=out_specs, check_vma=False
    )
```

```python
import functools
from types import SimpleNamespace

import jax
import jax.numpy as jnp
from jax import lax
from jax.experimental import pallas as pl
from jax.experimental.pallas import tpu as pltpu
from jax.sharding import PartitionSpec as P

EPSILON = 1e-05
ROOT_HALF = 0.7071067811865476
GAUSS_PEAK = 0.3989422804014327
SIDE = 7
WINDOW = SIDE * SIDE
IMAGE = 4 * WINDOW
TOK = 208
PAD = 64
LANES = 128
ROWS = 4 * PAD
F32 = jnp.float32
BF16 = jnp.bfloat16
VMEM = pl.BlockSpec(memory_space=pltpu.VMEM)
MESH = pl.DeviceIdType.MESH
LIMIT = 60 * 1024 * 1024


def dot(left, right):
    return jnp.dot(left, right, preferred_element_type=F32)


def dot_t(left, right):
    return lax.dot_general(left, right, (((1,), (1,)), ((), ())), preferred_element_type=F32)


def t_dot(left, right):
    return lax.dot_general(left, right, (((0,), (0,)), ((), ())), preferred_element_type=F32)


def thirds(values):
    high = values.astype(BF16).astype(F32)
    rest = values - high
    middle = rest.astype(BF16).astype(F32)
    return jnp.concatenate([high, middle, rest - middle], axis=0).astype(BF16)


def unthird(values):
    count = values.shape[0] // 3
    return values[:count] + values[count:2 * count] + values[2 * count:]


def norm(values):
    center = jnp.mean(values, axis=-1, keepdims=True)
    shifted = values - center
    spread = jnp.mean(shifted * shifted, axis=-1, keepdims=True)
    inverse = lax.rsqrt(spread + EPSILON)
    return shifted * inverse, inverse


def norm_backward(upstream, gain, normed, inverse):
    scaled = upstream * gain
    return inverse * (
        scaled
        - jnp.mean(scaled, axis=-1, keepdims=True)
        - normed * jnp.mean(scaled * normed, axis=-1, keepdims=True)
    )


def head_mask(heads, width):
    size = width // heads
    head = lax.broadcasted_iota(jnp.int32, (heads, 1, width), 0)
    lane = lax.broadcasted_iota(jnp.int32, (heads, 1, width), 2)
    return (lane >= head * size) & (lane < (head + 1) * size)


def stack_heads(rows, mask):
    heads = mask.shape[0]
    wide = jnp.where(mask, rows.astype(F32)[None], 0.0)
    return wide.reshape(heads * rows.shape[0], rows.shape[1]).astype(BF16)


def fold_heads(stacked, mask):
    heads = mask.shape[0]
    split = stacked.reshape(heads, stacked.shape[0] // heads, stacked.shape[1])
    return jnp.sum(jnp.where(mask, split, 0.0), axis=0)


def softmax(scores):
    top = jnp.max(scores, axis=-1, keepdims=True)
    powers = jnp.exp(scores - top)
    return powers / jnp.sum(powers, axis=-1, keepdims=True)


def block_kernel(n, size, names, *refs):
    r = SimpleNamespace(**dict(zip(names, refs)))
    me = lax.axis_index("dp")
    row, col = lax.axis_index("row"), lax.axis_index("col")
    cores = lax.axis_size("col")
    parity, place = lax.rem(me, 2), me // 2
    peers = n // 2
    over_col, over_row = {"col": 1 - col}, {"row": 1 - row}
    pair = {"dp": me + 1 - 2 * parity}
    half, width, hid = r.x_in.shape[1], r.wp.shape[0], r.we.shape[1]
    heads, entries = r.table.shape
    scale = (width // heads) ** (-0.5)
    images = r.x_in.shape[0] // IMAGE
    slices = hid // half
    mine = row * cores + col
    theirs = (1 - row) * cores + col
    wide, block = size // 2, size // n
    chunks = r.o_f.shape[0] // size
    live = {}

    def peer_of(k):
        there = lax.rem(place + k, peers)
        return there, {"dp": 2 * there + parity}

    barrier = pltpu.get_barrier_semaphore()
    for device in [over_col, over_row, pair] + [peer_of(k)[1] for k in range(1, peers)]:
        pl.semaphore_signal(barrier, inc=1, device_id=device, device_id_type=MESH)

    def start(key, src, dst, device):
        index = len(live)
        live[key] = pltpu.make_async_remote_copy(
            src, dst, r.sems.at[0, index], r.sems.at[1, index], device, MESH
        )
        live[key].start()

    def arrived(*key):
        live[key].wait_recv()

    def tokens_of(image):
        return pl.ds(pl.multiple_of(image * TOK, 16), TOK)

    r.vec_own[...] = jnp.zeros_like(r.vec_own)
    r.cvec_own[...] = jnp.zeros_like(r.cvec_own)
    for k, ref in enumerate((r.gain1, r.shift1, r.bias_p, r.gain2, r.shift2, r.bias_r)):
        r.vec_own[k:k + 1] = ref[...]
    r.cvec_own[0:1] = r.bias_q[...]
    r.cvec_own[1:2] = r.bias_v[...]
    for k in range(slices):
        r.cvec_own[2 + k:3 + k] = r.bias_e[:, k * half:(k + 1) * half]
    pl.semaphore_wait(barrier, peers + 2)

    above = lax.rem(place, 2)
    along = {"dp": 2 * (place + 1 - 2 * above) + parity}
    weights = {
        "q": (r.wq, r.q_xo, r.q_ox, r.q_xx, 2, "x"),
        "p": (r.wp, r.p_xo, r.p_ox, r.p_xx, 1, "z"),
        "e": (r.we, r.e_xo, r.e_ox, r.e_xx, 2, "z"),
        "r": (r.wr, r.r_xo, r.r_ox, r.r_xx, 2, "x"),
    }

    def view(name, ref, kind, p):
        count = weights[name][4]
        rows = ref.shape[-2]
        step = rows // (4 * count)
        quarter = {
            "y": 2 * above + parity,
            "x": 2 * above + 1 - parity,
            "z": 2 * (1 - above) + parity,
            "d": 2 * (1 - above) + 1 - parity,
        }[kind]
        at = pl.ds(pl.multiple_of(quarter * (rows // 4) + p * step, step), step)
        return ref.at[:, at] if len(ref.shape) == 3 else ref.at[at]

    def fetch(name):
        oo, xo, ox = weights[name][:3]
        for p in range(weights[name][4]):
            start((name, "y", p), view(name, oo, "y", p), view(name, xo, "y", p), over_row)
        start((name, "c"), oo, ox, over_col)

    def across(name, kind, p):
        arrived(name, kind, p)
        xo, xx = weights[name][1], weights[name][3]
        start((name, "c" + kind, p), view(name, xo, kind, p), view(name, xx, kind, p), over_col)

    def relay_one(name):
        xo = weights[name][1]
        for p in range(weights[name][4]):
            own = view(name, xo, "y", p)
            arrived(name, "y", p)
            start((name, "x", p), own, own, pair)
            start((name, "z", p), own, own, along)
            start((name, "cy", p), own, view(name, weights[name][3], "y", p), over_col)

    def relay_two(name):
        first = weights[name][5]
        for p in range(weights[name][4]):
            got = view(name, weights[name][1], first, p)
            arrived(name, first, p)
            start((name, "d", p), got, got, along if first == "x" else pair)
            start((name, "c" + first, p), got, view(name, weights[name][3], first, p), over_col)

    def relay_three(name):
        second = "z" if weights[name][5] == "x" else "x"
        for kind in (second, "d"):
            for p in range(weights[name][4]):
                across(name, kind, p)

    def ready(name):
        arrived(name, "c")
        for kind in ("cy", "cx", "cz", "cd"):
            for p in range(weights[name][4]):
                arrived(name, kind, p)

    fetch("q")
    start(("vec",), r.vec_own, r.vec_oth, over_row)
    start(("cvec",), r.cvec_own, r.cvec_oth, over_col)
    spot = lax.broadcasted_iota(jnp.int32, (TOK, images * IMAGE), 1)
    line = lax.broadcasted_iota(jnp.int32, (TOK, images * IMAGE), 0)
    line = jnp.where(line < IMAGE, line, -IMAGE * images)
    for k in range(images):
        r.sel[k * TOK:(k + 1) * TOK] = jnp.where(spot == line + k * IMAGE, 1.0, 0.0).astype(BF16)
    place_in = lax.broadcasted_iota(jnp.int32, (ROWS, TOK), 0)
    spot = lax.broadcasted_iota(jnp.int32, (ROWS, TOK), 1)
    window, i = place_in >> 6, place_in & (PAD - 1)
    i_row = (i * 37) >> 8
    target = ((window >> 1) * SIDE + i_row) * (2 * SIDE) + (window & 1) * SIDE + i - SIDE * i_row
    target = jnp.where(i < WINDOW, target, -1)
    r.perm[...] = jnp.where(spot == target, 1.0, 0.0).astype(BF16)
    sel_mine, sel_theirs = r.sel[tokens_of(mine)], r.sel[tokens_of(theirs)]
    r.x_away[...] = dot(sel_theirs, r.x_in[...]).astype(BF16)
    start(("x",), r.x_away, r.x_oth, over_row)
    fetch("p")
    fetch("e")
    fetch("r")
    r.g_away[...] = dot(sel_theirs, r.g_in[...]).astype(BF16)
    start(("g",), r.g_away, r.g_oth, over_row)
    which = lax.broadcasted_iota(jnp.int32, (entries, LANES), 0)
    for k in range(WINDOW):
        r.hot[:, k * LANES:(k + 1) * LANES] = jnp.where(which == r.index[k:k + 1], 1.0, 0.0).astype(BF16)
    relay_one("q")
    spread = unthird(dot(thirds(r.table[...]), r.hot[...]))
    lane = lax.broadcasted_iota(jnp.int32, (heads, PAD), 1)
    r.b_own[...] = jnp.zeros_like(r.b_own)
    for k in range(WINDOW):
        r.b_own[pl.ds(k, heads, stride=PAD), :] = jnp.where(
            lane < WINDOW, spread[:, k * LANES:k * LANES + PAD], -1e30
        )
    start(("bias",), r.b_own, r.b_oth, over_col)
    relay_two("q")
    x_own = dot(sel_mine, r.x_in[...]).astype(BF16)
    grad_own = dot(sel_mine, r.g_in[...]).astype(BF16)
    mask = head_mask(heads, width)

    arrived("x")
    arrived("vec")
    rvec = jnp.concatenate([r.vec_own[...], r.vec_oth[...]], axis=1)
    x = dot(r.perm[...], jnp.concatenate([x_own, r.x_oth[...]], axis=1))
    normed, inverse_one = norm(x)
    r.n_one[...] = normed
    r.ln_one[...] = (normed * rvec[0:1] + rvec[1:2]).astype(BF16)
    relay_one("p")
    relay_three("q")
    relay_two("p")
    arrived("cvec")
    q_side = (r.wq, r.q_ox), (r.q_xo, r.q_xx)
    p_side = (r.wp, r.p_ox), (r.p_xo, r.p_xx)
    e_side = (r.we, r.e_ox), (r.e_xo, r.e_xx)
    r_side = (r.wr, r.r_ox), (r.r_xo, r.r_xx)
    bias_refs = (r.b_own, r.b_oth)
    cvecs = (r.cvec_own, r.cvec_oth)
    for b in range(2):
        cols = slice(b * width, (b + 1) * width)
        if b == 1:
            relay_three("p")
            relay_one("e")
            ready("q")
            arrived("bias")
        for s, out in enumerate((r.q, r.k, r.v)):
            linear = dot(r.ln_one[:, :half], q_side[0][b][s]) + dot(
                r.ln_one[:, half:], q_side[1][b][s]
            )
            if s == 0:
                linear = (linear + cvecs[b][0:1]) * scale
            if s == 2:
                linear = linear + cvecs[b][1:2]
            out[:, cols] = linear.astype(BF16)
        for w in range(4):
            rows = slice(w * PAD, (w + 1) * PAD)
            scores = dot_t(stack_heads(r.q[rows, cols], mask), r.k[rows, cols]) + bias_refs[b][...]
            probs = softmax(scores)
            r.probs[b * 4 + w] = probs
            r.mixed[rows, cols] = fold_heads(dot(probs.astype(BF16), r.v[rows, cols]), mask).astype(BF16)
    relay_two("e")
    relay_one("r")
    ready("p")
    parts = [
        dot(r.mixed[:, :width], p_side[a][0][...]) + dot(r.mixed[:, width:], p_side[a][1][...])
        for a in range(2)
    ]
    middle = x + jnp.concatenate(parts, axis=1) + rvec[2:3]
    r.middle[...] = middle
    normed_two, inverse_two = norm(middle)
    r.ln_two[...] = (normed_two * rvec[3:4] + rvec[4:5]).astype(BF16)
    relay_three("e")
    relay_two("r")
    arrived("g")
    grad = dot(r.perm[...], jnp.concatenate([grad_own, r.g_oth[...]], axis=1))
    r.grad[...] = grad.astype(BF16)
    relay_three("r")
    ready("e")
    ready("r")

    def rows_of(c):
        return slice(c * size, (c + 1) * size)

    begun, rowed = [0], [0]

    def away_done(blocks):
        while (begun[0] + 1) * size <= blocks * half:
            c = begun[0]
            start(("y", c), r.y_b.at[rows_of(c)], r.yr.at[rows_of(c)], over_col)
            start(("z", c), r.z_b.at[rows_of(c)], r.zr.at[rows_of(c)], over_col)
            begun[0] += 1

    def home_done(blocks):
        while (rowed[0] + 1) * size <= blocks * half:
            c = rowed[0]
            rows = rows_of(c)
            arrived("z", c)
            r.xb[rows] = (r.x_f[rows] + r.zr[rows].astype(F32)).astype(BF16)
            start(("r", c), r.xb.at[rows], r.xr.at[rows], over_row)
            rowed[0] += 1

    def stage_pair(c):
        arrived("y", c)
        arrived("r", c)
        rows = rows_of(c)
        r.sf[...] = r.o_f[rows] + r.yr[rows].astype(F32) + r.xr[rows].astype(F32)
        r.sb[rows] = r.sf[...].astype(BF16)
        r.tf[c] = r.sf[pl.ds(pl.multiple_of(parity * wide, wide), wide)]
        away = pl.ds(pl.multiple_of(c * size + (1 - parity) * wide, wide), wide)
        start(("p", c), r.sb.at[away], r.pr.at[c], pair)

    def stage_rest(c):
        arrived("p", c)
        r.tf[c] = r.tf[c] + r.pr[c].astype(F32)
        r.tb[c] = r.tf[c].astype(BF16)
        for k in range(1, peers):
            there, device = peer_of(k)
            piece = pl.ds(pl.multiple_of(there * block, block), block)
            start(("q", c, k), r.tb.at[c, piece], r.qr.at[c, k], device)

    def stage_sum(c):
        total = r.tf[c, pl.ds(pl.multiple_of(place * block, block), block)]
        for k in range(1, peers):
            arrived("q", c, k)
            total = total + r.qr[c, k].astype(F32)
        own = pl.ds(pl.multiple_of(c * size + parity * wide + place * block, block), block)
        r.gb[own] = total.astype(BF16)
        for k in range(1, peers):
            start(("g", c, k), r.gb.at[own], r.gb.at[own], peer_of(k)[1])

    def stage_back(c):
        for k in range(1, peers):
            arrived("g", c, k)
        part = pl.ds(pl.multiple_of(c * size + parity * wide, wide), wide)
        start(("b", c), r.gb.at[part], r.gb.at[part], pair)

    def stage_out(c):
        arrived("b", c)

    drain = 2.9 * size / 256
    hop = 1.8 + drain / 2
    stages = (stage_pair, stage_rest, stage_sum, stage_back, stage_out)
    pending = sorted(
        (2.6 + drain * (c + 1) + hop * k, c, k) for c in range(chunks) for k in range(len(stages))
    )

    def advance(until):
        while pending and pending[0][0] <= until:
            _, c, k = pending[0]
            if k == 0 and c >= rowed[0]:
                return
            stages[k](c)
            pending.pop(0)

    homes, aways = (r.o_f, r.x_f), (r.y_b, r.z_b)
    r.small[...] = jnp.zeros_like(r.small)
    for q in range(slices):
        here = slice(q * half, (q + 1) * half)
        for b in (1, 0):
            cols = slice(b * hid + q * half, b * hid + (q + 1) * half)
            pre = dot(r.ln_two[:, :half], e_side[0][b][:, here]) + dot(
                r.ln_two[:, half:], e_side[1][b][:, here]
            )
            pre = pre + cvecs[b][2 + q:3 + q]
            erf_half = 0.5 * (1.0 + lax.erf(pre * ROOT_HALF))
            hidden = (pre * erf_half).astype(BF16)
            r.hidden[:, cols] = hidden
            slope = erf_half + pre * GAUSS_PEAK * jnp.exp(-0.5 * pre * pre)
            hgrad = dot_t(r.grad[:, :half], r_side[0][b][here]) + dot_t(
                r.grad[:, half:], r_side[1][b][here]
            )
            pgrad = (hgrad * slope).astype(BF16)
            r.pg[:, cols] = pgrad
            at = (32 if b == 0 else 16) + 2 + q
            r.small[at:at + 1] = jnp.sum(pgrad.astype(F32), axis=0, keepdims=True)
            up = slice(2 * q * half, (2 * q + 1) * half)
            down = slice((2 * q + 1) * half, (2 * q + 2) * half)
            for a, out in enumerate(homes if b == 0 else aways):
                side = slice(a * half, (a + 1) * half)
                out[up] = t_dot(r.ln_two[:, side], pgrad).astype(out.dtype)
                out[down] = t_dot(hidden, r.grad[:, side]).astype(out.dtype)
            if b == 1:
                away_done(2 * q + 2)
        home_done(2 * q + 2)
    advance(6.5)
    second = jnp.concatenate(
        [
            dot_t(r.pg[:, :hid], e_side[a][0][...]) + dot_t(r.pg[:, hid:], e_side[a][1][...])
            for a in range(2)
        ],
        axis=1,
    )
    mgrad = r.grad[...].astype(F32) + norm_backward(second, rvec[3:4], normed_two, inverse_two)
    r.mgrad[...] = mgrad
    r.mid_b[...] = mgrad.astype(BF16)
    for k, values in ((2, mgrad), (3, second * normed_two), (4, second), (5, r.grad[...].astype(F32))):
        total = jnp.sum(values, axis=0, keepdims=True)
        r.small[k:k + 1] = total[:, :half]
        r.small[8 + k:9 + k] = total[:, half:]
    base = 2 * slices * half
    for b in (1, 0):
        cols = slice(b * width, (b + 1) * width)
        r.mg[:, cols] = (
            dot_t(r.mid_b[:, :half], p_side[0][b][...]) + dot_t(r.mid_b[:, half:], p_side[1][b][...])
        ).astype(BF16)
        for a, out in enumerate(homes if b == 0 else aways):
            out[base:base + half] = t_dot(
                r.mixed[:, cols], r.mid_b[:, a * half:(a + 1) * half]
            ).astype(out.dtype)
    away_done(2 * slices + 1)

    def spread_out(key, values, out):
        tokens = t_dot(r.perm[...], values.astype(BF16)).astype(BF16)
        r.t_own[key] = tokens[:, :half]
        r.t_away[key] = tokens[:, half:]
        start(("o0", key), r.t_own.at[key], out.at[tokens_of(mine)], over_col)
        start(("o1", key), r.t_away.at[key], out.at[tokens_of(mine)], over_row)
        out[tokens_of(mine)] = tokens[:, :half]

    def pass_on(key, out):
        arrived("o1", key)
        start(("o2", key), out.at[tokens_of(theirs)], out.at[tokens_of(theirs)], over_col)

    def collect(key, out, result):
        arrived("o0", key)
        arrived("o2", key)
        result[...] = t_dot(r.sel[...], out[...]).astype(result.dtype)

    parts = [
        dot(r.hidden[:, :hid], r_side[a][0][...]) + dot(r.hidden[:, hid:], r_side[a][1][...])
        for a in range(2)
    ]
    home_done(2 * slices + 1)
    spread_out(0, r.middle[...] + jnp.concatenate(parts, axis=1) + rvec[5:6], r.t_blk)
    advance(9)

    for b in (1, 0):
        cols = slice(b * width, (b + 1) * width)
        small = 32 if b == 0 else 16
        q_sum = jnp.zeros((1, width), F32)
        v_sum = jnp.zeros((1, width), F32)
        for w in range(4):
            rows = slice(w * PAD, (w + 1) * PAD)
            keys, values = r.k[rows, cols], r.v[rows, cols]
            q_stack = stack_heads(r.q[rows, cols], mask)
            g_stack = stack_heads(r.mg[rows, cols], mask)
            probs = r.probs[b * 4 + w]
            pgrad = dot_t(g_stack, values)
            sgrad = probs * (pgrad - jnp.sum(probs * pgrad, axis=-1, keepdims=True))
            r.bg[b] = sgrad if w == 0 else r.bg[b] + sgrad
            score_b = sgrad.astype(BF16)
            q_grad = fold_heads(dot(score_b, keys), mask) * scale
            k_grad = t_dot(score_b, q_stack)
            v_grad = t_dot(probs.astype(BF16), g_stack)
            q_sum = q_sum + jnp.sum(q_grad, axis=0, keepdims=True)
            v_sum = v_sum + jnp.sum(v_grad, axis=0, keepdims=True)
            r.lin[b, rows, 0:width] = q_grad.astype(BF16)
            r.lin[b, rows, width:2 * width] = k_grad.astype(BF16)
            r.lin[b, rows, 2 * width:3 * width] = v_grad.astype(BF16)
        r.small[small:small + 1] = q_sum
        r.small[small + 1:small + 2] = v_sum
        for s in range(3):
            part = r.lin[b, :, s * width:(s + 1) * width]
            at = base + (s + 1) * half
            for a, out in enumerate(homes if b == 0 else aways):
                out[at:at + half] = t_dot(r.ln_one[:, a * half:(a + 1) * half], part).astype(out.dtype)
            if b == 1:
                away_done(2 * slices + 2 + s)
            else:
                home_done(2 * slices + 2 + s)
        advance(12 if b == 1 else 15)
    first = jnp.concatenate(
        [
            sum(
                dot_t(r.lin[b, :, s * width:(s + 1) * width], q_side[a][b][s])
                for b in range(2)
                for s in range(3)
            )
            for a in range(2)
        ],
        axis=1,
    )
    for k, values in ((0, first * r.n_one[...]), (1, first)):
        total = jnp.sum(values, axis=0, keepdims=True)
        r.small[k:k + 1] = total[:, :half]
        r.small[8 + k:9 + k] = total[:, half:]
    r.flat[...] = jnp.zeros_like(r.flat)
    for b in range(2):
        for k in range(WINDOW):
            r.flat[b * heads:(b + 1) * heads, k * LANES:k * LANES + PAD] = r.bg[
                b, pl.ds(k, heads, stride=PAD), :
            ]
    table_grad = unthird(dot_t(thirds(r.flat[...]), r.hot[...]))
    r.small[40:48, 0:entries] = table_grad[:heads]
    r.small[24:32, 0:entries] = table_grad[heads:]
    start(("s0",), r.small.at[0:32], r.s_col, over_col)
    in_grad = r.mgrad[...] + norm_backward(first, rvec[0:1], r.n_one[...], inverse_one)
    spread_out(1, in_grad, r.t_in)
    advance(18)
    pass_on(0, r.t_blk)
    arrived("s0")
    r.s_mid[0:8] = r.small[8:16] + r.s_col[8:16]
    r.s_mid[8:24] = r.small[32:48] + r.s_col[16:32]
    start(("s1",), r.s_mid, r.s_row, over_row)
    advance(22)
    collect(0, r.t_blk, r.out_b)
    late = 2.6 + drain * chunks
    advance(late)
    arrived("s1")
    r.s_pair[0:8] = r.small[0:8] + r.s_col[0:8] + r.s_row[0:8]
    r.s_pair[8:24] = r.s_mid[8:24] + r.s_row[8:24]
    start(("s2",), r.s_pair, r.s_other, pair)
    advance(late + 3.5)
    pass_on(1, r.t_in)
    arrived("s2")
    r.s_dp[place] = r.s_pair[...] + r.s_other[...]
    for k in range(1, peers):
        start(("s3", k), r.s_dp.at[place], r.s_dp.at[place], peer_of(k)[1])
    advance(late + 7)
    collect(1, r.t_in, r.out_x)
    for k in range(1, peers):
        arrived("s3", k)
    acc = r.s_dp[0]
    for k in range(1, peers):
        acc = acc + r.s_dp[k]
    r.sums[...] = acc
    advance(1e9)
    for key, copy in live.items():
        copy.wait_send()


def deliver_kernel(slices, gb, out_b, out_x, sums, *refs):
    outs, sems = refs[:16], refs[-1]
    held = refs[16:-1]
    half = gb.shape[1]
    copies = []

    def send(at, src, dst):
        copies.append(pltpu.make_async_copy(src, dst, sems.at[at]))
        copies[-1].start()

    send(0, out_b, outs[0])
    for q in range(slices):
        cols = slice(q * half, (q + 1) * half)
        held[0][:, cols] = gb[2 * q * half:(2 * q + 1) * half].astype(F32)
    send(1, held[0], outs[12])
    for q in range(slices):
        held[1][q * half:(q + 1) * half] = gb[(2 * q + 1) * half:(2 * q + 2) * half].astype(F32)
    send(2, held[1], outs[14])
    held[2][...] = out_x[...].astype(F32)
    send(3, held[2], outs[1])
    base = 2 * slices * half
    for s in range(3):
        held[3][s] = gb[base + (s + 1) * half:base + (s + 2) * half].astype(F32)
    send(4, held[3], outs[4])
    held[4][...] = gb[base:base + half].astype(F32)
    send(5, held[4], outs[8])
    for k, at in enumerate((2, 3, 9, 10, 11, 15)):
        outs[at][...] = sums[k:k + 1]
    outs[5][...] = sums[8:9]
    outs[6][...] = sums[9:10]
    for k in range(slices):
        outs[13][:, k * half:(k + 1) * half] = sums[10 + k:11 + k]
    heads, entries = outs[7].shape
    outs[7][...] = sums[16:16 + heads, 0:entries]
    for copy in copies:
        copy.wait()


def per_device(
    block_input, out_grad, first_gain, first_shift, qkv_weight, query_bias, value_bias,
    position_table, position_index, proj_weight, proj_bias, second_gain, second_shift,
    expand_weight, expand_bias, reduce_weight, reduce_bias,
):
    n = lax.axis_size("dp")
    half = block_input.shape[1]
    width = qkv_weight.shape[2]
    hid = expand_weight.shape[1]
    entries, heads = position_table.shape
    slices = hid // half
    images = block_input.shape[0] // IMAGE
    full = 2 * half
    rows = 2 * hid + 4 * half
    size = max(n * 16, half)
    chunks, peers, wide = rows // size, n // 2, size // 2
    index = jnp.pad(position_index, ((0, 0), (0, LANES - WINDOW)), constant_values=-1)
    inputs = dict(
        x_in=block_input, g_in=out_grad,
        gain1=first_gain[None], shift1=first_shift[None], bias_p=proj_bias[None],
        gain2=second_gain[None], shift2=second_shift[None], bias_r=reduce_bias[None],
        bias_q=query_bias[None], bias_v=value_bias[None], bias_e=expand_bias[None],
        table=position_table.T, index=index,
        wq=qkv_weight.transpose(1, 0, 2), wp=proj_weight, we=expand_weight, wr=reduce_weight,
    )
    outputs = dict(
        gb=((rows, half), BF16), out_b=(block_input.shape, BF16), out_x=(block_input.shape, BF16),
        sums=((24, half), F32),
    )
    scratch = dict(
        sel=((images * TOK, images * IMAGE), BF16), perm=((ROWS, TOK), BF16),
        x_away=((TOK, half), BF16), x_oth=((TOK, half), BF16),
        g_away=((TOK, half), BF16), g_oth=((TOK, half), BF16),
        vec_own=((8, half), F32), vec_oth=((8, half), F32),
        cvec_own=((8, half), F32), cvec_oth=((8, half), F32),
        hot=((entries, WINDOW * LANES), BF16),
        b_own=((heads * PAD, PAD), F32), b_oth=((heads * PAD, PAD), F32),
        n_one=((ROWS, full), F32), ln_one=((ROWS, full), BF16),
        q=((ROWS, full), BF16), k=((ROWS, full), BF16), v=((ROWS, full), BF16),
        mixed=((ROWS, full), BF16), probs=((8, heads * PAD, PAD), F32),
        middle=((ROWS, full), F32), ln_two=((ROWS, full), BF16), grad=((ROWS, full), BF16),
        hidden=((ROWS, 2 * hid), BF16), pg=((ROWS, 2 * hid), BF16),
        mgrad=((ROWS, full), F32), mid_b=((ROWS, full), BF16), mg=((ROWS, full), BF16),
        lin=((2, ROWS, 3 * width), BF16), bg=((2, heads * PAD, PAD), F32),
        flat=((2 * heads, WINDOW * LANES), F32),
        t_own=((2, TOK, half), BF16), t_away=((2, TOK, half), BF16),
        t_blk=((images * TOK, half), BF16), t_in=((images * TOK, half), BF16),
        o_f=((rows, half), F32), x_f=((rows, half), F32),
        y_b=((rows, half), BF16), z_b=((rows, half), BF16),
        yr=((rows, half), BF16), zr=((rows, half), BF16),
        xb=((rows, half), BF16), xr=((rows, half), BF16), sb=((rows, half), BF16),
        sf=((size, half), F32),
        pr=((chunks, wide, half), BF16), tb=((chunks, wide, half), BF16),
        tf=((chunks, wide, half), F32), qr=((chunks, peers, size // n, half), BF16),
        small=((48, half), F32), s_col=((32, half), F32), s_mid=((24, half), F32),
        s_row=((24, half), F32), s_pair=((24, half), F32), s_other=((24, half), F32),
        s_dp=((peers, 24, half), F32),
    )
    for name, weight in (("q", "wq"), ("p", "wp"), ("e", "we"), ("r", "wr")):
        for side in ("xo", "ox", "xx"):
            scratch[name + "_" + side] = (inputs[weight].shape, BF16)
    copies = 96 + chunks * (5 + 2 * (peers - 1)) + peers
    names = list(inputs) + list(outputs) + list(scratch) + ["sems"]
    results = pl.pallas_call(
        functools.partial(block_kernel, n, size, names),
        name="block",
        out_shape=tuple(jax.ShapeDtypeStruct(*out) for out in outputs.values()),
        in_specs=[VMEM] * len(inputs),
        out_specs=tuple([VMEM] * len(outputs)),
        scratch_shapes=[pltpu.VMEM(*shape) for shape in scratch.values()]
        + [pltpu.SemaphoreType.DMA((2, copies))],
        compiler_params=pltpu.CompilerParams(
            collective_id=0, has_side_effects=True, vmem_limit_bytes=LIMIT
        ),
    )(*inputs.values())
    line, big = pl.BlockSpec(memory_space=pltpu.VMEM), pl.BlockSpec(memory_space=pl.ANY)
    vec = jax.ShapeDtypeStruct((1, half), F32)
    tokens = block_input.shape
    held = [(half, hid), (hid, half), tokens, (3, half, width), (width, half)]
    shape = jax.ShapeDtypeStruct
    final = pl.pallas_call(
        functools.partial(deliver_kernel, slices),
        name="deliver",
        out_shape=(
            shape(tokens, BF16), shape(tokens, F32), vec, vec, shape(held[3], F32), vec, vec,
            shape((heads, entries), F32), shape(held[4], F32), vec, vec, vec,
            shape(held[0], F32), shape((1, hid), F32), shape(held[1], F32), vec,
        ),
        in_specs=[VMEM] * 4,
        out_specs=(big, big, line, line, big, line, line, line, big, line, line, line, big, line, big, line),
        scratch_shapes=[pltpu.VMEM(h, F32) for h in held] + [pltpu.SemaphoreType.DMA((6,))],
    )(*results)
    final = list(final)
    for at in (2, 3, 5, 6, 9, 10, 11, 13, 15):
        final[at] = final[at][0]
    final[4] = final[4].transpose(1, 0, 2)
    final[7] = final[7].T
    return tuple(final)


def solution(mesh):
    in_specs = (
        P("dp", "row"), P("dp", "row"), P("row"), P("row"), P("row", None, "col"), P("col"),
        P("col"), P(None, "col"), P(), P("col", "row"), P("row"), P("row"), P("row"),
        P("row", "col"), P("col"), P("col", "row"), P("row"),
    )
    out_specs = (
        P("dp", "row"), P("dp", "row"), P("row"), P("row"), P("row", None, "col"), P("col"),
        P("col"), P(None, "col"), P("col", "row"), P("row"), P("row"), P("row"),
        P("row", "col"), P("col"), P("col", "row"), P("row"),
    )
    return jax.shard_map(
        per_device, mesh=mesh, in_specs=in_specs, out_specs=out_specs, check_vma=False
    )
```

```python
import functools
from types import SimpleNamespace

import jax
import jax.numpy as jnp
from jax import lax
from jax.experimental import pallas as pl
from jax.experimental.pallas import tpu as pltpu
from jax.sharding import PartitionSpec as P

EPSILON = 1e-05
ROOT_HALF = 0.7071067811865476
GAUSS_PEAK = 0.3989422804014327
SIDE = 7
WINDOW = SIDE * SIDE
IMAGE = 4 * WINDOW
TOK = 208
PAD = 64
LANES = 128
ROWS = 4 * PAD
F32 = jnp.float32
BF16 = jnp.bfloat16
VMEM = pl.BlockSpec(memory_space=pltpu.VMEM)
MESH = pl.DeviceIdType.MESH
LIMIT = 60 * 1024 * 1024


def dot(left, right):
    return jnp.dot(left, right, preferred_element_type=F32)


def dot_t(left, right):
    return lax.dot_general(left, right, (((1,), (1,)), ((), ())), preferred_element_type=F32)


def t_dot(left, right):
    return lax.dot_general(left, right, (((0,), (0,)), ((), ())), preferred_element_type=F32)


def thirds(values):
    high = values.astype(BF16).astype(F32)
    rest = values - high
    middle = rest.astype(BF16).astype(F32)
    return jnp.concatenate([high, middle, rest - middle], axis=0).astype(BF16)


def unthird(values):
    count = values.shape[0] // 3
    return values[:count] + values[count:2 * count] + values[2 * count:]


def norm(values):
    center = jnp.mean(values, axis=-1, keepdims=True)
    shifted = values - center
    spread = jnp.mean(shifted * shifted, axis=-1, keepdims=True)
    inverse = lax.rsqrt(spread + EPSILON)
    return shifted * inverse, inverse


def norm_backward(upstream, gain, normed, inverse):
    scaled = upstream * gain
    return inverse * (
        scaled
        - jnp.mean(scaled, axis=-1, keepdims=True)
        - normed * jnp.mean(scaled * normed, axis=-1, keepdims=True)
    )


def head_mask(heads, width):
    size = width // heads
    head = lax.broadcasted_iota(jnp.int32, (heads, 1, width), 0)
    lane = lax.broadcasted_iota(jnp.int32, (heads, 1, width), 2)
    return (lane >= head * size) & (lane < (head + 1) * size)


def stack_heads(rows, mask):
    heads = mask.shape[0]
    wide = jnp.where(mask, rows.astype(F32)[None], 0.0)
    return wide.reshape(heads * rows.shape[0], rows.shape[1]).astype(BF16)


def fold_heads(stacked, mask):
    heads = mask.shape[0]
    split = stacked.reshape(heads, stacked.shape[0] // heads, stacked.shape[1])
    return jnp.sum(jnp.where(mask, split, 0.0), axis=0)


def softmax(scores):
    top = jnp.max(scores, axis=-1, keepdims=True)
    powers = jnp.exp(scores - top)
    return powers / jnp.sum(powers, axis=-1, keepdims=True)


def block_kernel(n, size, names, *refs):
    r = SimpleNamespace(**dict(zip(names, refs)))
    me = lax.axis_index("dp")
    row, col = lax.axis_index("row"), lax.axis_index("col")
    cores = lax.axis_size("col")
    parity, place = lax.rem(me, 2), me // 2
    peers = n // 2
    over_col, over_row = {"col": 1 - col}, {"row": 1 - row}
    pair = {"dp": me + 1 - 2 * parity}
    half, width, hid = r.x_in.shape[1], r.wp.shape[0], r.we.shape[1]
    heads, entries = r.table.shape
    scale = (width // heads) ** (-0.5)
    images = r.x_in.shape[0] // IMAGE
    slices = hid // half
    mine = row * cores + col
    theirs = (1 - row) * cores + col
    wide, block = size // 2, size // n
    chunks = r.o_f.shape[0] // size
    live = {}

    def peer_of(k):
        there = lax.rem(place + k, peers)
        return there, {"dp": 2 * there + parity}

    barrier = pltpu.get_barrier_semaphore()
    for device in [over_col, over_row, pair] + [peer_of(k)[1] for k in range(1, peers)]:
        pl.semaphore_signal(barrier, inc=1, device_id=device, device_id_type=MESH)

    loads = {
        name: pltpu.make_async_copy(getattr(r, "in_" + name), getattr(r, name), r.loads.at[k])
        for k, name in enumerate(at[3:] for at in names if at.startswith("in_"))
    }
    for copy in loads.values():
        copy.start()

    def start(key, src, dst, device):
        index = len(live)
        live[key] = pltpu.make_async_remote_copy(
            src, dst, r.sems.at[0, index], r.sems.at[1, index], device, MESH
        )
        live[key].start()

    def arrived(*key):
        live[key].wait_recv()

    def tokens_of(image):
        return pl.ds(pl.multiple_of(image * TOK, 16), TOK)

    for copy in loads.values():
        copy.wait()
    r.vec_own[...] = jnp.zeros_like(r.vec_own)
    r.cvec_own[...] = jnp.zeros_like(r.cvec_own)
    for k, ref in enumerate((r.gain1, r.shift1, r.bias_p, r.gain2, r.shift2, r.bias_r)):
        r.vec_own[k:k + 1] = ref[...]
    r.cvec_own[0:1] = r.bias_q[...]
    r.cvec_own[1:2] = r.bias_v[...]
    for k in range(slices):
        r.cvec_own[2 + k:3 + k] = r.bias_e[:, k * half:(k + 1) * half]
    pl.semaphore_wait(barrier, peers + 2)

    above = lax.rem(place, 2)
    along = {"dp": 2 * (place + 1 - 2 * above) + parity}
    weights = {
        "q": (r.wq, r.q_xo, r.q_ox, r.q_xx, 2, "x"),
        "p": (r.wp, r.p_xo, r.p_ox, r.p_xx, 1, "z"),
        "e": (r.we, r.e_xo, r.e_ox, r.e_xx, 2, "z"),
        "r": (r.wr, r.r_xo, r.r_ox, r.r_xx, 2, "x"),
    }

    def view(name, ref, kind, p):
        count = weights[name][4]
        rows = ref.shape[-2]
        step = rows // (4 * count)
        quarter = {
            "y": 2 * above + parity,
            "x": 2 * above + 1 - parity,
            "z": 2 * (1 - above) + parity,
            "d": 2 * (1 - above) + 1 - parity,
        }[kind]
        at = pl.ds(pl.multiple_of(quarter * (rows // 4) + p * step, step), step)
        return ref.at[:, at] if len(ref.shape) == 3 else ref.at[at]

    def fetch(name):
        oo, xo, ox = weights[name][:3]
        for p in range(weights[name][4]):
            start((name, "y", p), view(name, oo, "y", p), view(name, xo, "y", p), over_row)
        start((name, "c"), oo, ox, over_col)

    def across(name, kind, p):
        arrived(name, kind, p)
        xo, xx = weights[name][1], weights[name][3]
        start((name, "c" + kind, p), view(name, xo, kind, p), view(name, xx, kind, p), over_col)

    def relay_one(name):
        xo = weights[name][1]
        for p in range(weights[name][4]):
            own = view(name, xo, "y", p)
            arrived(name, "y", p)
            start((name, "x", p), own, own, pair)
            start((name, "z", p), own, own, along)
            start((name, "cy", p), own, view(name, weights[name][3], "y", p), over_col)

    def relay_two(name):
        first = weights[name][5]
        for p in range(weights[name][4]):
            got = view(name, weights[name][1], first, p)
            arrived(name, first, p)
            start((name, "d", p), got, got, along if first == "x" else pair)
            start((name, "c" + first, p), got, view(name, weights[name][3], first, p), over_col)

    def relay_three(name):
        second = "z" if weights[name][5] == "x" else "x"
        for kind in (second, "d"):
            for p in range(weights[name][4]):
                across(name, kind, p)

    def ready(name):
        arrived(name, "c")
        for kind in ("cy", "cx", "cz", "cd"):
            for p in range(weights[name][4]):
                arrived(name, kind, p)

    fetch("q")
    start(("vec",), r.vec_own, r.vec_oth, over_row)
    start(("cvec",), r.cvec_own, r.cvec_oth, over_col)
    spot = lax.broadcasted_iota(jnp.int32, (TOK, images * IMAGE), 1)
    line = lax.broadcasted_iota(jnp.int32, (TOK, images * IMAGE), 0)
    line = jnp.where(line < IMAGE, line, -IMAGE * images)
    for k in range(images):
        r.sel[k * TOK:(k + 1) * TOK] = jnp.where(spot == line + k * IMAGE, 1.0, 0.0).astype(BF16)
    place_in = lax.broadcasted_iota(jnp.int32, (ROWS, TOK), 0)
    spot = lax.broadcasted_iota(jnp.int32, (ROWS, TOK), 1)
    window, i = place_in >> 6, place_in & (PAD - 1)
    i_row = (i * 37) >> 8
    target = ((window >> 1) * SIDE + i_row) * (2 * SIDE) + (window & 1) * SIDE + i - SIDE * i_row
    target = jnp.where(i < WINDOW, target, -1)
    r.perm[...] = jnp.where(spot == target, 1.0, 0.0).astype(BF16)
    sel_mine, sel_theirs = r.sel[tokens_of(mine)], r.sel[tokens_of(theirs)]
    r.x_away[...] = dot(sel_theirs, r.x_in[...]).astype(BF16)
    start(("x",), r.x_away, r.x_oth, over_row)
    fetch("p")
    fetch("e")
    fetch("r")
    r.g_away[...] = dot(sel_theirs, r.g_in[...]).astype(BF16)
    start(("g",), r.g_away, r.g_oth, over_row)
    which = lax.broadcasted_iota(jnp.int32, (entries, WINDOW), 0)
    r.hot[...] = jnp.zeros_like(r.hot)
    for k in range(WINDOW):
        r.hot[:, k * LANES:k * LANES + WINDOW] = jnp.where(which == r.index[k:k + 1], 1.0, 0.0).astype(BF16)
    relay_one("q")
    spread = unthird(dot(thirds(r.table[...]), r.hot[...]))
    lane = lax.broadcasted_iota(jnp.int32, (heads, PAD), 1)
    r.b_own[...] = jnp.zeros_like(r.b_own)
    for k in range(WINDOW):
        r.b_own[pl.ds(k, heads, stride=PAD), :] = jnp.where(
            lane < WINDOW, spread[:, k * LANES:k * LANES + PAD], -1e30
        )
    start(("bias",), r.b_own, r.b_oth, over_col)
    relay_two("q")
    x_own = dot(sel_mine, r.x_in[...]).astype(BF16)
    grad_own = dot(sel_mine, r.g_in[...]).astype(BF16)
    mask = head_mask(heads, width)

    arrived("x")
    arrived("vec")
    rvec = jnp.concatenate([r.vec_own[...], r.vec_oth[...]], axis=1)
    x = dot(r.perm[...], jnp.concatenate([x_own, r.x_oth[...]], axis=1))
    normed, inverse_one = norm(x)
    r.n_one[...] = normed
    r.ln_one[...] = (normed * rvec[0:1] + rvec[1:2]).astype(BF16)
    relay_one("p")
    relay_one("e")
    relay_three("q")
    relay_two("p")
    arrived("cvec")
    q_side = (r.wq, r.q_ox), (r.q_xo, r.q_xx)
    p_side = (r.wp, r.p_ox), (r.p_xo, r.p_xx)
    e_side = (r.we, r.e_ox), (r.e_xo, r.e_xx)
    r_side = (r.wr, r.r_ox), (r.r_xo, r.r_xx)
    bias_refs = (r.b_own, r.b_oth)
    cvecs = (r.cvec_own, r.cvec_oth)
    for b in range(2):
        cols = slice(b * width, (b + 1) * width)
        if b == 1:
            relay_one("r")
            ready("q")
            arrived("bias")
        for s, out in enumerate((r.q, r.k, r.v)):
            linear = dot(r.ln_one[:, :half], q_side[0][b][s]) + dot(
                r.ln_one[:, half:], q_side[1][b][s]
            )
            if s == 0:
                linear = (linear + cvecs[b][0:1]) * scale
            if s == 2:
                linear = linear + cvecs[b][1:2]
            out[:, cols] = linear.astype(BF16)
        for w in range(4):
            rows = slice(w * PAD, (w + 1) * PAD)
            scores = dot_t(stack_heads(r.q[rows, cols], mask), r.k[rows, cols]) + bias_refs[b][...]
            probs = softmax(scores)
            r.probs[b * 4 + w] = probs
            r.mixed[rows, cols] = fold_heads(dot(probs.astype(BF16), r.v[rows, cols]), mask).astype(BF16)
    relay_three("p")
    relay_two("e")
    ready("p")
    parts = [
        dot(r.mixed[:, :width], p_side[a][0][...]) + dot(r.mixed[:, width:], p_side[a][1][...])
        for a in range(2)
    ]
    middle = x + jnp.concatenate(parts, axis=1) + rvec[2:3]
    r.middle[...] = middle
    normed_two, inverse_two = norm(middle)
    r.ln_two[...] = (normed_two * rvec[3:4] + rvec[4:5]).astype(BF16)
    relay_two("r")
    relay_three("e")
    arrived("g")
    grad = dot(r.perm[...], jnp.concatenate([grad_own, r.g_oth[...]], axis=1))
    r.grad[...] = grad.astype(BF16)
    relay_three("r")
    ready("e")
    ready("r")

    def rows_of(c):
        return slice(c * size, (c + 1) * size)

    begun, rowed = [0], [0]

    def away_done(blocks):
        while (begun[0] + 1) * size <= blocks * half:
            c = begun[0]
            start(("y", c), r.y_b.at[rows_of(c)], r.yr.at[rows_of(c)], over_col)
            start(("z", c), r.z_b.at[rows_of(c)], r.zr.at[rows_of(c)], over_col)
            begun[0] += 1

    def home_done(blocks):
        while (rowed[0] + 1) * size <= blocks * half:
            c = rowed[0]
            rows = rows_of(c)
            arrived("z", c)
            r.xb[rows] = (r.x_f[rows] + r.zr[rows].astype(F32)).astype(BF16)
            start(("r", c), r.xb.at[rows], r.xr.at[rows], over_row)
            rowed[0] += 1

    def stage_pair(c):
        arrived("y", c)
        arrived("r", c)
        rows = rows_of(c)
        r.sf[...] = r.o_f[rows] + r.yr[rows].astype(F32) + r.xr[rows].astype(F32)
        r.sb[rows] = r.sf[...].astype(BF16)
        r.tf[c] = r.sf[pl.ds(pl.multiple_of(parity * wide, wide), wide)]
        away = pl.ds(pl.multiple_of(c * size + (1 - parity) * wide, wide), wide)
        start(("p", c), r.sb.at[away], r.pr.at[c], pair)

    def stage_rest(c):
        arrived("p", c)
        r.tf[c] = r.tf[c] + r.pr[c].astype(F32)
        r.tb[c] = r.tf[c].astype(BF16)
        for k in range(1, peers):
            there, device = peer_of(k)
            piece = pl.ds(pl.multiple_of(there * block, block), block)
            start(("q", c, k), r.tb.at[c, piece], r.qr.at[c, k], device)

    def stage_sum(c):
        total = r.tf[c, pl.ds(pl.multiple_of(place * block, block), block)]
        for k in range(1, peers):
            arrived("q", c, k)
            total = total + r.qr[c, k].astype(F32)
        own = pl.ds(pl.multiple_of(c * size + parity * wide + place * block, block), block)
        r.gb[own] = total.astype(BF16)
        for k in range(1, peers):
            start(("g", c, k), r.gb.at[own], r.gb.at[own], peer_of(k)[1])

    def stage_back(c):
        for k in range(1, peers):
            arrived("g", c, k)
        part = pl.ds(pl.multiple_of(c * size + parity * wide, wide), wide)
        start(("b", c), r.gb.at[part], r.gb.at[part], pair)

    def stage_out(c):
        arrived("b", c)

    drain = 2.9 * size / 256
    hop = 1.8 + drain / 2
    stages = (stage_pair, stage_rest, stage_sum, stage_back, stage_out)
    pending = sorted(
        (2.6 + drain * (c + 1) + hop * k, c, k) for c in range(chunks) for k in range(len(stages))
    )

    def advance(until):
        while pending and pending[0][0] <= until:
            _, c, k = pending[0]
            if k == 0 and c >= rowed[0]:
                return
            stages[k](c)
            pending.pop(0)

    homes, aways = (r.o_f, r.x_f), (r.y_b, r.z_b)
    r.small[...] = jnp.zeros_like(r.small)
    for q in range(slices):
        here = slice(q * half, (q + 1) * half)
        for b in (1, 0):
            cols = slice(b * hid + q * half, b * hid + (q + 1) * half)
            pre = dot(r.ln_two[:, :half], e_side[0][b][:, here]) + dot(
                r.ln_two[:, half:], e_side[1][b][:, here]
            )
            pre = pre + cvecs[b][2 + q:3 + q]
            erf_half = 0.5 * (1.0 + lax.erf(pre * ROOT_HALF))
            hidden = (pre * erf_half).astype(BF16)
            r.hidden[:, cols] = hidden
            slope = erf_half + pre * GAUSS_PEAK * jnp.exp(-0.5 * pre * pre)
            hgrad = dot_t(r.grad[:, :half], r_side[0][b][here]) + dot_t(
                r.grad[:, half:], r_side[1][b][here]
            )
            pgrad = (hgrad * slope).astype(BF16)
            r.pg[:, cols] = pgrad
            at = (32 if b == 0 else 16) + 2 + q
            r.small[at:at + 1] = jnp.sum(pgrad.astype(F32), axis=0, keepdims=True)
            up = slice(2 * q * half, (2 * q + 1) * half)
            down = slice((2 * q + 1) * half, (2 * q + 2) * half)
            for a, out in enumerate(homes if b == 0 else aways):
                side = slice(a * half, (a + 1) * half)
                out[up] = t_dot(r.ln_two[:, side], pgrad).astype(out.dtype)
                out[down] = t_dot(hidden, r.grad[:, side]).astype(out.dtype)
            if b == 1:
                away_done(2 * q + 2)
                home_done(2 * q)
        if q in (0, slices - 1):
            home_done(2 * q + 2)
    advance(9)
    second = jnp.concatenate(
        [
            dot_t(r.pg[:, :hid], e_side[a][0][...]) + dot_t(r.pg[:, hid:], e_side[a][1][...])
            for a in range(2)
        ],
        axis=1,
    )
    mgrad = r.grad[...].astype(F32) + norm_backward(second, rvec[3:4], normed_two, inverse_two)
    r.mgrad[...] = mgrad
    r.mid_b[...] = mgrad.astype(BF16)
    for k, values in ((2, mgrad), (3, second * normed_two), (4, second), (5, r.grad[...].astype(F32))):
        total = jnp.sum(values, axis=0, keepdims=True)
        r.small[k:k + 1] = total[:, :half]
        r.small[8 + k:9 + k] = total[:, half:]
    base = 2 * slices * half
    for b in (1, 0):
        cols = slice(b * width, (b + 1) * width)
        r.mg[:, cols] = (
            dot_t(r.mid_b[:, :half], p_side[0][b][...]) + dot_t(r.mid_b[:, half:], p_side[1][b][...])
        ).astype(BF16)
        for a, out in enumerate(homes if b == 0 else aways):
            out[base:base + half] = t_dot(
                r.mixed[:, cols], r.mid_b[:, a * half:(a + 1) * half]
            ).astype(out.dtype)
    away_done(2 * slices + 1)

    def spread_out(key, values, out):
        tokens = t_dot(r.perm[...], values.astype(BF16)).astype(BF16)
        r.t_own[key] = tokens[:, :half]
        r.t_away[key] = tokens[:, half:]
        start(("o0", key), r.t_own.at[key], out.at[tokens_of(mine)], over_col)
        start(("o1", key), r.t_away.at[key], out.at[tokens_of(mine)], over_row)
        out[tokens_of(mine)] = tokens[:, :half]

    def pass_on(key, out):
        arrived("o1", key)
        start(("o2", key), out.at[tokens_of(theirs)], out.at[tokens_of(theirs)], over_col)

    def collect(key, out, result):
        arrived("o0", key)
        arrived("o2", key)
        result[...] = t_dot(r.sel[...], out[...]).astype(result.dtype)

    parts = [
        dot(r.hidden[:, :hid], r_side[a][0][...]) + dot(r.hidden[:, hid:], r_side[a][1][...])
        for a in range(2)
    ]
    home_done(2 * slices + 1)
    spread_out(0, r.middle[...] + jnp.concatenate(parts, axis=1) + rvec[5:6], r.t_blk)
    advance(12)

    for b in (1, 0):
        cols = slice(b * width, (b + 1) * width)
        small = 32 if b == 0 else 16
        q_sum = jnp.zeros((1, width), F32)
        v_sum = jnp.zeros((1, width), F32)
        for w in range(4):
            rows = slice(w * PAD, (w + 1) * PAD)
            keys, values = r.k[rows, cols], r.v[rows, cols]
            q_stack = stack_heads(r.q[rows, cols], mask)
            g_stack = stack_heads(r.mg[rows, cols], mask)
            probs = r.probs[b * 4 + w]
            pgrad = dot_t(g_stack, values)
            sgrad = probs * (pgrad - jnp.sum(probs * pgrad, axis=-1, keepdims=True))
            r.bg[b] = sgrad if w == 0 else r.bg[b] + sgrad
            score_b = sgrad.astype(BF16)
            q_grad = fold_heads(dot(score_b, keys), mask) * scale
            k_grad = t_dot(score_b, q_stack)
            v_grad = t_dot(probs.astype(BF16), g_stack)
            q_sum = q_sum + jnp.sum(q_grad, axis=0, keepdims=True)
            v_sum = v_sum + jnp.sum(v_grad, axis=0, keepdims=True)
            r.lin[b, rows, 0:width] = q_grad.astype(BF16)
            r.lin[b, rows, width:2 * width] = k_grad.astype(BF16)
            r.lin[b, rows, 2 * width:3 * width] = v_grad.astype(BF16)
        r.small[small:small + 1] = q_sum
        r.small[small + 1:small + 2] = v_sum
        for s in range(3):
            part = r.lin[b, :, s * width:(s + 1) * width]
            at = base + (s + 1) * half
            for a, out in enumerate(homes if b == 0 else aways):
                out[at:at + half] = t_dot(r.ln_one[:, a * half:(a + 1) * half], part).astype(out.dtype)
            if b == 1:
                away_done(2 * slices + 2 + s)
            else:
                home_done(2 * slices + 2 + s)
        advance(16 if b == 1 else 20)
    first = jnp.concatenate(
        [
            sum(
                dot_t(r.lin[b, :, s * width:(s + 1) * width], q_side[a][b][s])
                for b in range(2)
                for s in range(3)
            )
            for a in range(2)
        ],
        axis=1,
    )
    for k, values in ((0, first * r.n_one[...]), (1, first)):
        total = jnp.sum(values, axis=0, keepdims=True)
        r.small[k:k + 1] = total[:, :half]
        r.small[8 + k:9 + k] = total[:, half:]
    r.flat[...] = jnp.zeros_like(r.flat)
    for b in range(2):
        for k in range(WINDOW):
            r.flat[b * heads:(b + 1) * heads, k * LANES:k * LANES + PAD] = r.bg[
                b, pl.ds(k, heads, stride=PAD), :
            ]
    table_grad = unthird(dot_t(thirds(r.flat[...]), r.hot[...]))
    r.small[40:48, 0:entries] = table_grad[:heads]
    r.small[24:32, 0:entries] = table_grad[heads:]
    start(("s0",), r.small.at[0:32], r.s_col, over_col)
    in_grad = r.mgrad[...] + norm_backward(first, rvec[0:1], r.n_one[...], inverse_one)
    spread_out(1, in_grad, r.t_in)
    advance(24)
    pass_on(0, r.t_blk)
    arrived("s0")
    r.s_mid[0:8] = r.small[8:16] + r.s_col[8:16]
    r.s_mid[8:24] = r.small[32:48] + r.s_col[16:32]
    start(("s1",), r.s_mid, r.s_row, over_row)
    advance(30)
    collect(0, r.t_blk, r.out_b)
    late = 2.6 + drain * chunks
    advance(late)
    arrived("s1")
    r.s_pair[0:8] = r.small[0:8] + r.s_col[0:8] + r.s_row[0:8]
    r.s_pair[8:24] = r.s_mid[8:24] + r.s_row[8:24]
    start(("s2",), r.s_pair, r.s_other, pair)
    advance(late + 3.5)
    pass_on(1, r.t_in)
    arrived("s2")
    r.s_dp[place] = r.s_pair[...] + r.s_other[...]
    for k in range(1, peers):
        start(("s3", k), r.s_dp.at[place], r.s_dp.at[place], peer_of(k)[1])
    advance(late + 7)
    collect(1, r.t_in, r.out_x)
    for k in range(1, peers):
        arrived("s3", k)
    acc = r.s_dp[0]
    for k in range(1, peers):
        acc = acc + r.s_dp[k]
    r.sums[...] = acc
    advance(1e9)
    for key, copy in live.items():
        copy.wait_send()


def deliver_kernel(slices, gb, out_b, out_x, sums, *refs):
    outs, sems = refs[:16], refs[-1]
    held = refs[16:-1]
    half = gb.shape[1]
    copies = []

    def send(at, src, dst):
        copies.append(pltpu.make_async_copy(src, dst, sems.at[at]))
        copies[-1].start()

    send(0, out_b, outs[0])
    for q in range(slices):
        cols = slice(q * half, (q + 1) * half)
        held[0][:, cols] = gb[2 * q * half:(2 * q + 1) * half].astype(F32)
    send(1, held[0], outs[12])
    for q in range(slices):
        held[1][q * half:(q + 1) * half] = gb[(2 * q + 1) * half:(2 * q + 2) * half].astype(F32)
    send(2, held[1], outs[14])
    held[2][...] = out_x[...].astype(F32)
    send(3, held[2], outs[1])
    base = 2 * slices * half
    for s in range(3):
        held[3][s] = gb[base + (s + 1) * half:base + (s + 2) * half].astype(F32)
    send(4, held[3], outs[4])
    held[4][...] = gb[base:base + half].astype(F32)
    send(5, held[4], outs[8])
    for k, at in enumerate((2, 3, 9, 10, 11, 15)):
        outs[at][...] = sums[k:k + 1]
    outs[5][...] = sums[8:9]
    outs[6][...] = sums[9:10]
    for k in range(slices):
        outs[13][:, k * half:(k + 1) * half] = sums[10 + k:11 + k]
    heads, entries = outs[7].shape
    outs[7][...] = sums[16:16 + heads, 0:entries]
    for copy in copies:
        copy.wait()


def per_device(
    block_input, out_grad, first_gain, first_shift, qkv_weight, query_bias, value_bias,
    position_table, position_index, proj_weight, proj_bias, second_gain, second_shift,
    expand_weight, expand_bias, reduce_weight, reduce_bias,
):
    n = lax.axis_size("dp")
    half = block_input.shape[1]
    width = qkv_weight.shape[2]
    hid = expand_weight.shape[1]
    entries, heads = position_table.shape
    slices = hid // half
    images = block_input.shape[0] // IMAGE
    full = 2 * half
    rows = 2 * hid + 4 * half
    size = max(n * 16, half)
    chunks, peers, wide = rows // size, n // 2, size // 2
    inputs = dict(
        x_in=block_input, g_in=out_grad,
        gain1=first_gain[None], shift1=first_shift[None], bias_p=proj_bias[None],
        gain2=second_gain[None], shift2=second_shift[None], bias_r=reduce_bias[None],
        bias_q=query_bias[None], bias_v=value_bias[None], bias_e=expand_bias[None],
        table=position_table.T, index=position_index,
        wq=qkv_weight.transpose(1, 0, 2), wp=proj_weight, we=expand_weight, wr=reduce_weight,
    )
    outputs = dict(
        gb=((rows, half), BF16), out_b=(block_input.shape, BF16), out_x=(block_input.shape, BF16),
        sums=((24, half), F32),
    )
    scratch = dict(
        sel=((images * TOK, images * IMAGE), BF16), perm=((ROWS, TOK), BF16),
        x_away=((TOK, half), BF16), x_oth=((TOK, half), BF16),
        g_away=((TOK, half), BF16), g_oth=((TOK, half), BF16),
        vec_own=((8, half), F32), vec_oth=((8, half), F32),
        cvec_own=((8, half), F32), cvec_oth=((8, half), F32),
        hot=((entries, WINDOW * LANES), BF16),
        b_own=((heads * PAD, PAD), F32), b_oth=((heads * PAD, PAD), F32),
        n_one=((ROWS, full), F32), ln_one=((ROWS, full), BF16),
        q=((ROWS, full), BF16), k=((ROWS, full), BF16), v=((ROWS, full), BF16),
        mixed=((ROWS, full), BF16), probs=((8, heads * PAD, PAD), F32),
        middle=((ROWS, full), F32), ln_two=((ROWS, full), BF16), grad=((ROWS, full), BF16),
        hidden=((ROWS, 2 * hid), BF16), pg=((ROWS, 2 * hid), BF16),
        mgrad=((ROWS, full), F32), mid_b=((ROWS, full), BF16), mg=((ROWS, full), BF16),
        lin=((2, ROWS, 3 * width), BF16), bg=((2, heads * PAD, PAD), F32),
        flat=((2 * heads, WINDOW * LANES), F32),
        t_own=((2, TOK, half), BF16), t_away=((2, TOK, half), BF16),
        t_blk=((images * TOK, half), BF16), t_in=((images * TOK, half), BF16),
        o_f=((rows, half), F32), x_f=((rows, half), F32),
        y_b=((rows, half), BF16), z_b=((rows, half), BF16),
        yr=((rows, half), BF16), zr=((rows, half), BF16),
        xb=((rows, half), BF16), xr=((rows, half), BF16), sb=((rows, half), BF16),
        sf=((size, half), F32),
        pr=((chunks, wide, half), BF16), tb=((chunks, wide, half), BF16),
        tf=((chunks, wide, half), F32), qr=((chunks, peers, size // n, half), BF16),
        small=((48, half), F32), s_col=((32, half), F32), s_mid=((24, half), F32),
        s_row=((24, half), F32), s_pair=((24, half), F32), s_other=((24, half), F32),
        s_dp=((peers, 24, half), F32),
    )
    for name, weight in (("q", "wq"), ("p", "wp"), ("e", "we"), ("r", "wr")):
        for side in ("xo", "ox", "xx"):
            scratch[name + "_" + side] = (inputs[weight].shape, BF16)
    copies = 96 + chunks * (5 + 2 * (peers - 1)) + peers
    for name, value in inputs.items():
        scratch[name] = (value.shape, value.dtype)
    names = ["in_" + name for name in inputs] + list(outputs) + list(scratch) + ["loads", "sems"]
    results = pl.pallas_call(
        functools.partial(block_kernel, n, size, names),
        name="block",
        out_shape=tuple(jax.ShapeDtypeStruct(*out) for out in outputs.values()),
        in_specs=[pl.BlockSpec(memory_space=pltpu.HBM)] * len(inputs),
        out_specs=tuple([VMEM] * len(outputs)),
        scratch_shapes=[pltpu.VMEM(*shape) for shape in scratch.values()]
        + [pltpu.SemaphoreType.DMA((len(inputs),)), pltpu.SemaphoreType.DMA((2, copies))],
        compiler_params=pltpu.CompilerParams(
            collective_id=0, has_side_effects=True, vmem_limit_bytes=LIMIT
        ),
    )(*inputs.values())
    line, big = pl.BlockSpec(memory_space=pltpu.VMEM), pl.BlockSpec(memory_space=pl.ANY)
    vec = jax.ShapeDtypeStruct((1, half), F32)
    tokens = block_input.shape
    held = [(half, hid), (hid, half), tokens, (3, half, width), (width, half)]
    shape = jax.ShapeDtypeStruct
    final = pl.pallas_call(
        functools.partial(deliver_kernel, slices),
        name="deliver",
        out_shape=(
            shape(tokens, BF16), shape(tokens, F32), vec, vec, shape(held[3], F32), vec, vec,
            shape((heads, entries), F32), shape(held[4], F32), vec, vec, vec,
            shape(held[0], F32), shape((1, hid), F32), shape(held[1], F32), vec,
        ),
        in_specs=[VMEM] * 4,
        out_specs=(big, big, line, line, big, line, line, line, big, line, line, line, big, line, big, line),
        scratch_shapes=[pltpu.VMEM(h, F32) for h in held] + [pltpu.SemaphoreType.DMA((6,))],
    )(*results)
    final = list(final)
    for at in (2, 3, 5, 6, 9, 10, 11, 13, 15):
        final[at] = final[at][0]
    final[4] = final[4].transpose(1, 0, 2)
    final[7] = final[7].T
    return tuple(final)


def solution(mesh):
    in_specs = (
        P("dp", "row"), P("dp", "row"), P("row"), P("row"), P("row", None, "col"), P("col"),
        P("col"), P(None, "col"), P(), P("col", "row"), P("row"), P("row"), P("row"),
        P("row", "col"), P("col"), P("col", "row"), P("row"),
    )
    out_specs = (
        P("dp", "row"), P("dp", "row"), P("row"), P("row"), P("row", None, "col"), P("col"),
        P("col"), P(None, "col"), P("col", "row"), P("row"), P("row"), P("row"),
        P("row", "col"), P("col"), P("col", "row"), P("row"),
    )
    return jax.shard_map(
        per_device, mesh=mesh, in_specs=in_specs, out_specs=out_specs, check_vma=False
    )
```
